128 devices in a mesh: band: 32 (over z, x, core), sector: 4 (over y).
Axes of the slice: x: 4, y: 4, z: 4, core: 2. Of those that a mesh axis runs over, the one named last changes fastest.
Arguments:
- node_latent: bfloat16 [65536, 256], P(('band', 'sector')), may hold values from -6 to 6
- edge_latent: bfloat16 [786432, 256], P(('band', 'sector')), may hold values from -6 to 6
- sender_slot: int32 [65536, 12], P(('band', 'sector')), may hold values from 0 to 1023, as said below
- edge_mask: int32 [65536, 12], P(('band', 'sector')), may hold values 0 or 1
- send_rows: int32 [128, 8, 64], P(('band', 'sector')), may hold values from 0 to 511
- w_edge_in: bfloat16 [768, 256], replicated, may hold values from -0.21875 to 0.21875
- b_edge: float32 [256], replicated, may hold values from -3 to 3
- w_edge_out: bfloat16 [256, 256], replicated, may hold values from -0.375 to 0.375
- g_edge: float32 [256], replicated, may hold values from 0.1 to 1.9
- w_node_in: bfloat16 [512, 256], replicated, may hold values from -0.25 to 0.25
- b_node: float32 [256], replicated, may hold values from -3 to 3
- w_node_out: bfloat16 [256, 256], replicated, may hold values from -0.375 to 0.375
- g_node: float32 [256], replicated, may hold values from 0.1 to 1.9
- node_cot: bfloat16 [65536, 256], P(('band', 'sector')), may hold values from -6 to 6
- edge_cot: bfloat16 [786432, 256], P(('band', 'sector')), may hold values from -6 to 6
Outputs:
- node_new: bfloat16 [65536, 256], P(('band', 'sector'))
- edge_new: bfloat16 [786432, 256], P(('band', 'sector'))
- node_grad: float32 [65536, 256], P(('band', 'sector'))
- edge_grad: bfloat16 [786432, 256], P(('band', 'sector'))
- grad_edge_in: float32 [768, 256], replicated
- grad_edge_out: float32 [256, 256], replicated
- grad_node_in: float32 [512, 256], replicated
- grad_node_out: float32 [256, 256], replicated
The draws below stay inside these ranges and needn't reach their ends.
Inputs may be any that keep to these rules, and one draw needn't show every extreme that they name: `sender_slot`: values below 512 name the receiver owner's own nodes; value 512 + j * 64 + c names row send_rows[q, j, c] of the neighbouring owner q in direction j; directions that would leave the first or last band never occur.
All inputs are finite; a program needn't handle non-finite values. No bound on the sum of `edge_mask` on one device may be relied on, other than what follows from the above.
Results may differ from the reference program's by a relative error of at most 0.013.
Values may be sent and summed in bfloat16 or wider, within the bound.
A program may use at most 128 MiB of HBM per device.

```python
import jax
import jax.numpy as jnp
from jax import lax

D = 256
NODE_DEV = 512
K = 12
CAP = 64
NODES = 65536
EDGES = 786432
N_BAND = 32
N_SECTOR = 4


band_steps = (-1, -1, -1, 0, 0, 1, 1, 1)


def draw_sender_slot(key, part):
    first_key = jax.random.fold_in(key, 11)
    second_key = jax.random.fold_in(key, 12)
    third_key = jax.random.fold_in(key, 13)
    course = jax.random.randint(first_key, (NODES, K), 0, 9)
    column = jax.random.randint(second_key, (NODES, K), 0, CAP)
    local_row = jax.random.randint(third_key, (NODES, K), 0, NODE_DEV)
    owner = jnp.arange(NODES, dtype=jnp.int32) // NODE_DEV
    own_band = (owner // N_SECTOR)[:, None]
    band_table = jnp.array(band_steps + (0,), dtype=jnp.int32)
    far_band = own_band + band_table[course]
    valid = (course < 8) & (far_band >= 0) & (far_band < N_BAND)
    values = jnp.where(valid, NODE_DEV + course * CAP + column, local_row)
    leading = (jnp.arange(NODES, dtype=jnp.int32) % NODE_DEV == 0)[:, None]
    slot_index = jnp.arange(K, dtype=jnp.int32)[None, :]
    highest = jnp.where(own_band < N_BAND - 1, NODE_DEV + 8 * CAP - 1, NODE_DEV + 5 * CAP - 1)
    values = jnp.where(leading & (slot_index == 0), highest, values)
    values = jnp.where(leading & (slot_index == 1), 0, values)
    return values.astype(jnp.int32)


def touch_ends(drawn, own_key, least, top_value):
    index_at = [jax.random.randint(jax.random.fold_in(own_key, axis), (), 0, length) for axis, length in enumerate(drawn.shape)]
    widest = drawn.shape.index(max(drawn.shape))
    beside = index_at[:widest] + [(index_at[widest] + 1) % drawn.shape[widest]] + index_at[widest + 1:]
    return drawn.at[tuple(index_at)].set(least).at[tuple(beside)].set(top_value)


def level_of(key, extent, split, least, largest):
    factor_of, own = 1.0, jax.random.fold_in(key, 6)
    for axis_at, parts in split:
        steps = jnp.exp(jax.random.uniform(jax.random.fold_in(own, axis_at), (parts,), jnp.float32, least / len(split), largest / len(split)))
        factor_of = factor_of * jnp.repeat(steps, extent[axis_at] // parts).reshape([-1 if axis == axis_at else 1 for axis in range(len(extent))])
    return factor_of


def gaussian(key, extent, spread, limit, shards=(), kind=jnp.bfloat16):
    values = jax.random.normal(key, extent, jnp.float32) * spread
    if len(shards) > 0:
        values = level_of(key, extent, shards, -0.22, 0.18) * values
    return jnp.clip(values, min=-limit, max=limit).astype(kind)


def setup_inputs(seed: int = 0) -> dict:
    streams_of = jax.random.split(jax.random.key(seed), 16)
    return {
        "node_latent": gaussian(streams_of[0], (NODES, D), 1.0, 6.0, ((0, 128),)),
        "edge_latent": gaussian(streams_of[1], (EDGES, D), 1.0, 6.0, ((0, 128),)),
        "sender_slot": draw_sender_slot(jax.random.fold_in(streams_of[15], 71), 0),
        "edge_mask": touch_ends((jax.random.randint(streams_of[3], (NODES, K), 0, 3) < 2).astype(jnp.int32), jax.random.fold_in(streams_of[3], 1), 0, 1),
        "send_rows": touch_ends(jax.random.randint(streams_of[4], (N_BAND * N_SECTOR, 8, CAP), 0, NODE_DEV), jax.random.fold_in(streams_of[4], 1), 0, NODE_DEV - 1).astype(jnp.int32),
        "w_edge_in": gaussian(streams_of[5], (3 * D, D), (3 * D) ** -0.5, 0.21875),
        "b_edge": gaussian(streams_of[6], (D,), 0.5, 3.0, (), jnp.float32),
        "w_edge_out": gaussian(streams_of[7], (D, D), D ** -0.5, 0.375),
        "g_edge": jnp.clip(1.0 + 0.18 * jax.random.normal(streams_of[8], (D,), jnp.float32), 0.1, 1.9),
        "w_node_in": gaussian(streams_of[9], (2 * D, D), (2 * D) ** -0.5, 0.25),
        "b_node": gaussian(streams_of[10], (D,), 0.5, 3.0, (), jnp.float32),
        "w_node_out": gaussian(streams_of[11], (D, D), D ** -0.5, 0.375),
        "g_node": jnp.clip(1.0 + 0.18 * jax.random.normal(streams_of[12], (D,), jnp.float32), 0.1, 1.9),
        "node_cot": gaussian(streams_of[13], (NODES, D), 1.0, 6.0, ((0, 128),)),
        "edge_cot": gaussian(streams_of[14], (EDGES, D), 1.0, 6.0, ((0, 128),)),
    }


band_steps = (-1, -1, -1, 0, 0, 1, 1, 1)
sector_steps = (-1, 0, 1, -1, 1, -1, 0, 1)

def layer_norm(values, gain):
    average = lax.optimization_barrier(jnp.mean(values, -1, keepdims=True))
    centred = values - average
    variance = lax.optimization_barrier(jnp.mean(centred * centred, -1, keepdims=True))
    return centred * lax.rsqrt(variance + 1e-05) * gain

def interact(own_f, sender_f, edge_block, mask_f, w_edge_in, b_edge, w_edge_out, g_edge, w_node_in, b_node, w_node_out, g_node):
    latent_width = own_f.shape[1]
    node_count = own_f.shape[0]
    slot_count = sender_f.shape[0] // node_count
    own_rows = own_f.astype(jnp.bfloat16)
    sender = sender_f.astype(jnp.bfloat16)
    from_edge = jnp.dot(edge_block, w_edge_in[:latent_width], preferred_element_type=jnp.float32)
    from_sender = jnp.dot(sender, w_edge_in[latent_width:2 * latent_width], preferred_element_type=jnp.float32)
    from_receiver = jnp.dot(own_rows, w_edge_in[2 * latent_width:], preferred_element_type=jnp.float32)
    pre_edge = (from_edge + from_sender).reshape(node_count, slot_count, latent_width) + from_receiver[:, None, :] + b_edge
    hidden = jax.nn.silu(pre_edge).astype(jnp.bfloat16).reshape(node_count * slot_count, latent_width)
    update = layer_norm(jnp.dot(hidden, w_edge_out, preferred_element_type=jnp.float32), g_edge) * mask_f
    edge_new = (edge_block.astype(jnp.float32) + update).astype(jnp.bfloat16)
    gathered = update.reshape(node_count, slot_count, latent_width).sum(1).astype(jnp.bfloat16)
    pre_node = jnp.dot(own_rows, w_node_in[:latent_width], preferred_element_type=jnp.float32)
    pre_node = pre_node + jnp.dot(gathered, w_node_in[latent_width:], preferred_element_type=jnp.float32) + b_node
    hidden_node = jax.nn.silu(pre_node).astype(jnp.bfloat16)
    node_new = (own_f + layer_norm(jnp.dot(hidden_node, w_node_out, preferred_element_type=jnp.float32), g_node)).astype(jnp.bfloat16)
    return (node_new, edge_new)

def differentiate(own_f, sender_f, edge_block, mask_f, weights, node_cot, edge_cot):
    w_edge_in, b_edge, w_edge_out, g_edge, w_node_in, b_node, w_node_out, g_node = weights

    def local_layer(own_in, sender_in, edge_in, first_edge, second_edge, first_node, second_node):
        return interact(own_in, sender_in, edge_in, mask_f, first_edge, b_edge, second_edge, g_edge, first_node, b_node, second_node, g_node)
    results, pullback = jax.vjp(local_layer, own_f, sender_f, edge_block, w_edge_in, w_edge_out, w_node_in, w_node_out)
    return (results, pullback((node_cot, edge_cot)))

def reference(node_latent, edge_latent, sender_slot, edge_mask, send_rows, w_edge_in, b_edge, w_edge_out, g_edge, w_node_in, b_node, w_node_out, g_node, node_cot, edge_cot):
    node_count = NODE_DEV
    peer_count = N_BAND * N_SECTOR
    latent_width = D
    slot_count = K
    weights = (w_edge_in, b_edge, w_edge_out, g_edge, w_node_in, b_node, w_node_out, g_node)
    node_f = node_latent.astype(jnp.float32)
    band_table = jnp.array(band_steps, dtype=jnp.int32)
    sector_table = jnp.array(sector_steps, dtype=jnp.int32)

    def per_block(carried, block_data):
        node_total, weight_totals = carried
        owner_index, edge_block, slot_block, mask_block, node_part, edge_part = block_data
        first_row = owner_index * node_count
        own_band = owner_index // N_SECTOR
        own_sector = owner_index % N_SECTOR
        own_f = lax.dynamic_slice_in_dim(node_f, first_row, node_count, 0)
        slot_flat = slot_block.reshape(-1)
        remote = jnp.maximum(slot_flat - node_count, 0)
        course = jnp.minimum(remote // CAP, 7)
        column = remote % CAP
        far_band = jnp.clip(own_band + band_table[course], 0, N_BAND - 1)
        far_sector = (own_sector + sector_table[course]) % N_SECTOR
        neighbour = (far_band * N_SECTOR + far_sector).astype(jnp.int32)
        far_row = send_rows[neighbour, course, column]
        global_index = jnp.where(slot_flat < node_count, first_row + slot_flat, neighbour * node_count + far_row).astype(jnp.int32)
        sender_f = node_f[global_index]
        mask_f = mask_block.reshape(-1, 1).astype(jnp.float32)
        results, gradients = differentiate(own_f, sender_f, edge_block, mask_f, weights, node_part, edge_part)
        d_own, d_sender, d_edge, g_first, g_second, g_third, g_fourth = gradients
        node_total = node_total.at[global_index].add(d_sender)
        current = lax.dynamic_slice_in_dim(node_total, first_row, node_count, 0)
        node_total = lax.dynamic_update_slice_in_dim(node_total, current + d_own, first_row, 0)
        weight_totals = tuple((total + part.astype(jnp.float32) for total, part in zip(weight_totals, (g_first, g_second, g_third, g_fourth))))
        return ((node_total, weight_totals), (results[0], results[1], d_edge))
    block_inputs = (jnp.arange(peer_count, dtype=jnp.int32), edge_latent.reshape(peer_count, node_count * slot_count, latent_width), sender_slot.reshape(peer_count, node_count, slot_count), edge_mask.reshape(peer_count, node_count, slot_count), node_cot.reshape(peer_count, node_count, latent_width), edge_cot.reshape(peer_count, node_count * slot_count, latent_width))
    initial = (jnp.zeros((peer_count * node_count, latent_width), jnp.float32), tuple((jnp.zeros(matrix.shape, jnp.float32) for matrix in (w_edge_in, w_edge_out, w_node_in, w_node_out))))
    (node_grad, weight_totals), (node_new, edge_new, edge_grad) = lax.scan(per_block, initial, block_inputs)
    grad_scale = float(peer_count * node_count * slot_count) ** (-0.5)
    return (node_new.reshape(-1, latent_width), edge_new.reshape(-1, latent_width), node_grad, edge_grad.reshape(-1, latent_width), weight_totals[0] * grad_scale, weight_totals[1] * grad_scale, weight_totals[2] * grad_scale, weight_totals[3] * grad_scale)
```

```python
import functools
import jax
import jax.numpy as jnp
from jax import lax
from jax.experimental import pallas as pl
from jax.experimental.pallas import tpu as pltpu
from jax.sharding import PartitionSpec as P

F32, BF16 = jnp.float32, jnp.bfloat16
R = 64
D = 256


def dot(a, b):
    return jnp.dot(a, b, preferred_element_type=F32)


def dot_rows(a, b):
    return lax.dot_general(a, b, (((0,), (0,)), ((), ())), preferred_element_type=F32)


def silu_parts(pre):
    gate = 0.5 * jnp.tanh(0.5 * pre) + 0.5
    hidden = pre * gate
    return hidden, gate + hidden * (1.0 - gate)


def centred(matrix):
    return matrix - jnp.mean(matrix, 1, keepdims=True)


def flipped(matrix):
    return jnp.transpose(matrix.astype(F32)).astype(BF16)


def layer_kernel(
    tiles, slots,
    own_ref, far_ref, edge_ref, slot_ref, mask_ref,
    w_ein, b_e, w_eout, g_e, w_nin, b_n, w_nout, g_n, ncot_ref, ecot_ref,
    nnew_ref, enew_ref, egrad_ref, ngrad_ref, back_ref, grads_ref,
    x_ref, xt_ref, wcat_ref, weo_ref, weot_ref, wet_ref, recv_ref, parts_ref,
    sel_ref, selt_ref, hid_ref, dsil_ref, xh_ref, rm_ref, gath_ref, dgath_ref,
    acc_ref, gout_ref, gd_ref, down_ref, gnode_ref,
):
    t = pl.program_id(0)
    rows = R * slots
    n = own_ref.shape[0]
    table = n + far_ref.shape[0]
    seg = D + table

    @pl.when(t == 0)
    def _():
        e = lax.broadcasted_iota(jnp.int32, (rows, 128), 0)
        l = lax.broadcasted_iota(jnp.int32, (rows, 128), 1)
        r = jnp.where(l >= R, l - R, l)
        gap = e - slots * r
        inside = (gap >= 0) & (gap < slots)
        x_ref[:, seg : seg + 128] = jnp.where(inside, 1.0, 0.0).astype(BF16)
        ef = e.astype(F32)
        k = ef - slots * jnp.floor((ef + 0.5) * (1.0 / slots))
        lf = l.astype(F32)
        sel_ref[...] = jnp.where(lf == k, 32.0, 0.0) + jnp.where(lf == k + 12.0, 1.0, 0.0)
        e = lax.broadcasted_iota(jnp.int32, (R, rows), 1)
        r = lax.broadcasted_iota(jnp.int32, (R, rows), 0)
        gap = e - slots * r
        inside = (gap >= 0) & (gap < slots)
        xt_ref[seg : seg + R, :] = jnp.where(inside, 1.0, 0.0).astype(BF16)
        ef = lax.broadcasted_iota(jnp.int32, (32, rows), 1).astype(F32)
        lf = lax.broadcasted_iota(jnp.int32, (32, rows), 0).astype(F32)
        k = ef - slots * jnp.floor((ef + 0.5) * (1.0 / slots))
        selt_ref[...] = jnp.where(lf == k, 32.0, 0.0) + jnp.where(lf == k + 12.0, 1.0, 0.0)
        v = slot_ref[...] + 1024 * mask_ref[...]
        high = (v >> 5).astype(F32)
        low = (v & 31).astype(F32)
        parts_ref[...] = jnp.concatenate(
            [high, low, jnp.zeros((n, 128 - 2 * slots), F32)], axis=1
        ).astype(BF16)
        wcat_ref[0:D, :] = w_ein[0:D, :]
        wcat_ref[D : D + n, :] = dot(own_ref[...], w_ein[D : 2 * D, :]).astype(BF16)
        wcat_ref[D + n : seg, :] = dot(far_ref[...], w_ein[D : 2 * D, :]).astype(BF16)
        recv_ref[...] = dot(own_ref[...], w_ein[2 * D :, :]) + b_e[...]
        weo = centred(w_eout[...].astype(F32))
        weo_ref[...] = weo.astype(BF16)
        weot_ref[...] = jnp.transpose(weo).astype(BF16)
        wet_ref[...] = flipped(w_ein[0:D, :])
        acc_ref[...] = jnp.zeros_like(acc_ref)
        gout_ref[...] = jnp.zeros_like(gout_ref)

    @pl.when(t < tiles)
    def _():
        here = pl.ds(pl.multiple_of(t * rows, rows), rows)
        mine = pl.ds(pl.multiple_of(t * R, R), R)
        edges = edge_ref[...]
        x_ref[:, 0:D] = edges
        spread = dot(x_ref[:, seg : seg + R], parts_ref[mine, :])
        v = jnp.sum(spread * sel_ref[...], 1, keepdims=True)
        real = v >= 1024.0
        slot = jnp.where(real, v - 1024.0, v)
        lane = lax.broadcasted_iota(jnp.int32, (rows, D), 1).astype(F32).astype(BF16)
        for block in range(table // D):
            wanted = (slot - float(block * D)).astype(BF16)
            x_ref[:, D + block * D : 2 * D + block * D] = jnp.where(
                lane == wanted, jnp.ones((), BF16), jnp.zeros((), BF16)
            )
        recv = recv_ref[mine, :]
        high = recv.astype(BF16)
        wcat_ref[seg : seg + R, :] = high
        wcat_ref[seg + R : seg + 2 * R, :] = (recv - high.astype(F32)).astype(BF16)
        pre = dot(x_ref[...], wcat_ref[...])
        hidden, slope = silu_parts(pre)
        hidden = hidden.astype(BF16)
        hid_ref[here, :] = hidden
        dsil_ref[here, :] = slope.astype(BF16)
        c = dot(hidden, weo_ref[...])
        rstd = lax.rsqrt(jnp.mean(c * c, 1, keepdims=True) + 1e-05)
        normed = c * rstd
        keep = jnp.where(real, 1.0, 0.0)
        xh_ref[here, :] = normed.astype(BF16)
        rm_ref[here, :] = rstd * keep
        update = normed * g_e[...] * keep
        enew_ref[...] = (edges.astype(F32) + update).astype(BF16)
        gath_ref[mine, :] = dot(xt_ref[seg : seg + R, :], update.astype(BF16)).astype(BF16)

    @pl.when(t == tiles)
    def _():
        own = own_ref[...]
        gath = gath_ref[...]
        pre = dot(own, w_nin[0:D, :]) + dot(gath, w_nin[D:, :]) + b_n[...]
        hidden, slope = silu_parts(pre)
        hidden = hidden.astype(BF16)
        wno = centred(w_nout[...].astype(F32))
        c = dot(hidden, wno.astype(BF16))
        rstd = lax.rsqrt(jnp.mean(c * c, 1, keepdims=True) + 1e-05)
        normed = c * rstd
        nnew_ref[...] = (own.astype(F32) + normed * g_n[...]).astype(BF16)
        cot = ncot_ref[...].astype(F32)
        dx = cot * g_n[...]
        share = jnp.mean(dx * normed, 1, keepdims=True)
        dz = (rstd * (dx - normed * share)).astype(BF16)
        gnode_ref[2 * D : 3 * D, :] = centred(dot_rows(hidden, dz))
        dpre = (dot(dz, jnp.transpose(wno).astype(BF16)) * slope).astype(BF16)
        gnode_ref[0:D, :] = dot_rows(own, dpre)
        gnode_ref[D : 2 * D, :] = dot_rows(gath, dpre)
        down_ref[...] = cot + dot(dpre, flipped(w_nin[0:D, :]))
        dgath_ref[...] = dot(dpre, flipped(w_nin[D:, :])).astype(BF16)

    @pl.when(t > tiles)
    def _():
        u = t - tiles - 1
        here = pl.ds(pl.multiple_of(u * rows, rows), rows)
        mine = pl.ds(pl.multiple_of(u * R, R), R)
        cot = ecot_ref[...].astype(F32)
        spread = dot(x_ref[:, seg : seg + R], dgath_ref[mine, :])
        dx = (cot + spread) * g_e[...]
        normed = xh_ref[here, :].astype(F32)
        share = jnp.mean(dx * normed, 1, keepdims=True)
        dz = (rm_ref[here, :] * (dx - normed * share)).astype(BF16)
        gout_ref[...] += dot_rows(hid_ref[here, :], dz)
        dpre = (dot(dz, weot_ref[...]) * dsil_ref[here, :].astype(F32)).astype(BF16)
        egrad_ref[...] = (cot + dot(dpre, wet_ref[...])).astype(BF16)
        part = dot_rows(parts_ref[mine, 0:32], xt_ref[seg : seg + R, :])
        v = jnp.sum(part * selt_ref[...], 0, keepdims=True)
        slot = jnp.where(v >= 1024.0, v - 1024.0, v)
        xt_ref[0:D, :] = jnp.transpose(edge_ref[...])
        line = lax.broadcasted_iota(jnp.int32, (D, rows), 0).astype(F32).astype(BF16)
        for block in range(table // D):
            wanted = (slot - float(block * D)).astype(BF16)
            xt_ref[D + block * D : 2 * D + block * D, :] = jnp.where(
                line == wanted, jnp.ones((), BF16), jnp.zeros((), BF16)
            )
        acc_ref[...] += dot(xt_ref[0:seg, :], dpre)
        gd_ref[mine, :] = dot(xt_ref[seg : seg + R, :], dpre).astype(BF16)

    @pl.when(t == 2 * tiles)
    def _():
        own = own_ref[...]
        near = acc_ref[D : D + n, :].astype(BF16)
        far = acc_ref[D + n : seg, :].astype(BF16)
        wst = flipped(w_ein[D : 2 * D, :])
        back_ref[...] = dot(far, wst).astype(BF16).reshape(back_ref.shape)
        gd = gd_ref[...]
        ngrad_ref[...] = down_ref[...] + dot(near, wst) + dot(gd, flipped(w_ein[2 * D :, :]))
        g_s = dot_rows(own, near) + dot_rows(far_ref[...], far)
        g_r = dot_rows(own, gd)
        whole = [acc_ref[0:D, :], g_s, g_r, centred(gout_ref[...])]
        whole += [gnode_ref[i * D : (i + 1) * D, :] for i in range(3)]
        at = 0
        for piece in whole:
            for i in range(D // 16):
                for j in range(2):
                    grads_ref[at] = piece[16 * i : 16 * i + 16, 128 * j : 128 * j + 128].astype(BF16)
                    at += 1


def layer_call(node, far, edge, slot, mask, w_ein, b_e, w_eout, g_e, w_nin, b_n, w_nout, g_n, ncot, ecot):
    n, d = node.shape
    slots = slot.shape[1]
    rows = R * slots
    tiles = n // R
    table = n + far.shape[0]
    seg = d + table
    total = n * slots
    whole = pl.BlockSpec(memory_space=pltpu.VMEM)
    stream_e = pl.BlockSpec((rows, d), lambda t: (jnp.where(t < tiles, t, jnp.maximum(t - tiles - 1, 0)), 0))
    first = pl.BlockSpec((rows, d), lambda t: (jnp.minimum(t, tiles - 1), 0))
    second = pl.BlockSpec((rows, d), lambda t: (jnp.maximum(t - tiles - 1, 0), 0))
    tiles_all = 7 * (d // 16) * (d // 128)
    flops = 2 * total * d * (d * 8 + 2 * table)
    return pl.pallas_call(
        functools.partial(layer_kernel, tiles, slots),
        grid=(2 * tiles + 1,),
        in_specs=[whole, whole, stream_e] + [whole] * 11 + [second],
        out_specs=[whole, first, second, whole, whole, whole],
        out_shape=[
            jax.ShapeDtypeStruct((n, d), BF16),
            jax.ShapeDtypeStruct((total, d), BF16),
            jax.ShapeDtypeStruct((total, d), BF16),
            jax.ShapeDtypeStruct((n, d), F32),
            jax.ShapeDtypeStruct((8, far.shape[0] // 8, d), BF16),
            jax.ShapeDtypeStruct((tiles_all, 16, 128), BF16),
        ],
        scratch_shapes=[
            pltpu.VMEM((rows, seg + 2 * R), BF16),
            pltpu.VMEM((seg + R, rows), BF16),
            pltpu.VMEM((seg + 2 * R, d), BF16),
            pltpu.VMEM((d, d), BF16),
            pltpu.VMEM((d, d), BF16),
            pltpu.VMEM((d, d), BF16),
            pltpu.VMEM((n, d), F32),
            pltpu.VMEM((n, 128), BF16),
            pltpu.VMEM((rows, 128), F32),
            pltpu.VMEM((32, rows), F32),
            pltpu.VMEM((total, d), BF16),
            pltpu.VMEM((total, d), BF16),
            pltpu.VMEM((total, d), BF16),
            pltpu.VMEM((total, 1), F32),
            pltpu.VMEM((n, d), BF16),
            pltpu.VMEM((n, d), BF16),
            pltpu.VMEM((seg, d), F32),
            pltpu.VMEM((d, d), F32),
            pltpu.VMEM((n, d), BF16),
            pltpu.VMEM((n, d), F32),
            pltpu.VMEM((3 * d, d), F32),
        ],
        compiler_params=pltpu.CompilerParams(vmem_limit_bytes=56 * 1024 * 1024),
        cost_estimate=pl.CostEstimate(flops=flops, bytes_accessed=5 * total * d * 2, transcendentals=total * d),
    )(node, far, edge, slot, mask, w_ein, b_e.reshape(1, -1), w_eout, g_e.reshape(1, -1), w_nin, b_n.reshape(1, -1), w_nout, g_n.reshape(1, -1), ncot, ecot)

band_steps = (-1, -1, -1, 0, 0, 1, 1, 1)
sector_steps = (-1, 0, 1, -1, 1, -1, 0, 1)
MESH = pl.DeviceIdType.MESH


def neighbours(bands, sectors):
    band, sector = lax.axis_index("band"), lax.axis_index("sector")
    ahead = [
        (lax.rem(band + b + bands, bands), lax.rem(sector + s + sectors, sectors))
        for b, s in zip(band_steps, sector_steps)
    ]
    return ahead


def greet(places):
    barrier = pltpu.get_barrier_semaphore()
    for place in places:
        pl.semaphore_signal(barrier, inc=1, device_id=place, device_id_type=MESH)
    pl.semaphore_wait(barrier, len(places))


def picked(wanted, count):
    line = lax.broadcasted_iota(jnp.int32, (count, wanted.shape[1]), 0)
    return jnp.where(line == wanted, 1.0, 0.0).astype(BF16)


def fetch_kernel(bands, sectors, node_ref, rows_ref, far_ref, out_ref, send_sem, recv_sem):
    ahead = neighbours(bands, sectors)
    barrier = pltpu.get_barrier_semaphore()
    for place in ahead:
        pl.semaphore_signal(barrier, inc=1, device_id=place, device_id_type=MESH)
    node = node_ref[...]
    for j in range(8):
        choice = picked(rows_ref[0, j : j + 1, :], node.shape[0])
        out_ref[j] = dot_rows(choice, node).astype(BF16)
    pl.semaphore_wait(barrier, 8)
    copies = []
    for j in range(8):
        copies.append(
            pltpu.make_async_remote_copy(
                src_ref=out_ref.at[j],
                dst_ref=far_ref.at[j],
                send_sem=send_sem.at[j],
                recv_sem=recv_sem.at[j],
                device_id=ahead[7 - j],
                device_id_type=MESH,
            )
        )
        copies[-1].start()
    for copy in copies:
        copy.wait()


def fetch_call(bands, sectors, node, rows):
    cap, d = rows.shape[2], node.shape[1]
    whole = pl.BlockSpec(memory_space=pltpu.VMEM)
    return pl.pallas_call(
        functools.partial(fetch_kernel, bands, sectors),
        in_specs=[whole, whole],
        out_specs=whole,
        out_shape=jax.ShapeDtypeStruct((8, cap, d), BF16),
        scratch_shapes=[
            pltpu.VMEM((8, cap, d), BF16),
            pltpu.SemaphoreType.DMA((8,)),
            pltpu.SemaphoreType.DMA((8,)),
        ],
        compiler_params=pltpu.CompilerParams(collective_id=0, has_side_effects=True),
    )(node, rows)


def sum_kernel(
    bands, sectors, share, back_ref, grads_ref, arrived_ref, out_ref,
    half_ref, one_ref, two_ref, three_ref, first_in, second_in, third_in,
    send_sem, recv_sem, core_sem, back_send, back_recv,
):
    ahead = neighbours(bands, sectors)
    band, sector = lax.axis_index("band"), lax.axis_index("sector")
    core = lax.rem(band, 2)
    x = lax.rem(band // 2, 4)
    z = band // 8
    at = {"x": x, "y": sector, "z": z}

    def place(axis, index):
        if axis == "x":
            return ((z * 4 + index) * 2 + core, sector)
        if axis == "z":
            return ((index * 4 + x) * 2 + core, sector)
        return (band, index)

    def others(axis):
        return [lax.rem(at[axis] + i, 4) for i in (1, 2, 3)]

    sibling = (band + 1 - 2 * core, sector)
    peers = [place("x", i) for i in others("x")] + [place("z", i) for i in others("z")]
    peers += [place("y", lax.rem(sector + 2, 4))]
    greet(ahead + peers)

    returns = []
    core_copy = pltpu.make_async_remote_copy(
        src_ref=grads_ref.at[1 - core], dst_ref=half_ref,
        send_sem=core_sem.at[0], recv_sem=core_sem.at[1],
        device_id=sibling, device_id_type=MESH,
    )
    core_copy.start()
    for j in range(8):
        returns.append(
            pltpu.make_async_remote_copy(
                src_ref=back_ref.at[j], dst_ref=arrived_ref.at[j],
                send_sem=back_send.at[j], recv_sem=back_recv.at[j],
                device_id=ahead[j], device_id_type=MESH,
            )
        )
        returns[-1].start()

    orders = (("x", "y", "z"), ("y", "z", "x"), ("z", "x", "y"))
    starts = [16 * sum(share[:p]) for p in range(3)]

    def exchange(stage, p, axis, source, target):
        copies = []
        for i, other in enumerate(others(axis)):
            copies.append(
                pltpu.make_async_remote_copy(
                    src_ref=source(other, i), dst_ref=target(i),
                    send_sem=send_sem.at[stage, p, i], recv_sem=recv_sem.at[stage, p, i],
                    device_id=place(axis, other), device_id_type=MESH,
                )
            )
            copies[-1].start()
        return copies

    def finish(copies):
        for copy in copies:
            copy.wait()

    core_copy.wait()
    one_ref[...] = (grads_ref[core].astype(F32) + half_ref[...].astype(F32)).astype(BF16)

    live = []
    for p in range(3):
        m, axis = share[p], orders[p][0]
        live.append(exchange(
            0, p, axis,
            lambda other, i, p=p, m=m: one_ref.at[pl.ds(starts[p] + other * (4 * m), 4 * m)],
            lambda i, p=p, m=m: first_in.at[i, pl.ds(4 * sum(share[:p]), 4 * m)],
        ))
    for p in range(3):
        m, axis, low = share[p], orders[p][0], 4 * sum(share[:p])
        finish(live[p])
        total = one_ref[pl.ds(starts[p] + at[axis] * (4 * m), 4 * m)].astype(F32)
        for i in range(3):
            total += first_in[i, low : low + 4 * m].astype(F32)
        two_ref[low : low + 4 * m] = total.astype(BF16)
        live[p] = exchange(
            1, p, orders[p][1],
            lambda other, i, low=low, m=m: two_ref.at[pl.ds(low + other * m, m)],
            lambda i, p=p, m=m: second_in.at[i, pl.ds(sum(share[:p]), m)],
        )
    for p in range(3):
        m, axis, low, mid = share[p], orders[p][1], sum(share[:p]), 4 * sum(share[:p])
        finish(live[p])
        total = two_ref[pl.ds(mid + at[axis] * m, m)].astype(F32)
        for i in range(3):
            total += second_in[i, low : low + m].astype(F32)
        three_ref[low : low + m] = total.astype(BF16)
        third = orders[p][2]
        third_in[at[third], low : low + m] = total.astype(BF16)
        live[p] = exchange(
            2, p, third,
            lambda other, i, low=low, m=m: three_ref.at[pl.ds(low, m)],
            lambda i, low=low, m=m, third=third: third_in.at[at[third], pl.ds(low, m)],
        )
    for p in range(3):
        m, low = share[p], sum(share[:p])
        finish(live[p])
        total = third_in[0, low : low + m].astype(F32)
        for i in range(1, 4):
            total += third_in[i, low : low + m].astype(F32)
        spot = starts[p] + at[orders[p][0]] * (4 * m) + at[orders[p][1]] * m
        out_ref[core, pl.ds(spot, m)] = total.astype(BF16)
        live[p] = exchange(
            3, p, orders[p][1],
            lambda other, i, spot=spot, m=m: out_ref.at[core, pl.ds(spot, m)],
            lambda i, spot=spot, m=m: out_ref.at[core, pl.ds(spot, m)],
        )
    for p in range(3):
        m = share[p]
        finish(live[p])
        spot = starts[p] + at[orders[p][0]] * (4 * m)
        live[p] = exchange(
            4, p, orders[p][0],
            lambda other, i, spot=spot, m=m: out_ref.at[core, pl.ds(spot, 4 * m)],
            lambda i, spot=spot, m=m: out_ref.at[core, pl.ds(spot, 4 * m)],
        )
    last = []
    for p in range(3):
        finish(live[p])
        spot, m = starts[p], 16 * share[p]
        last.append(pltpu.make_async_remote_copy(
            src_ref=out_ref.at[core, pl.ds(spot, m)], dst_ref=out_ref.at[core, pl.ds(spot, m)],
            send_sem=core_sem.at[2 + p], recv_sem=core_sem.at[5 + p],
            device_id=sibling, device_id_type=MESH,
        ))
        last[-1].start()
    finish(returns)
    finish(last)


def sum_call(bands, sectors, back, grads):
    half = grads.shape[0] // 2
    unit = half // 16
    share = (unit - 2 * (unit // 3), unit // 3, unit // 3)
    whole = pl.BlockSpec(memory_space=pltpu.VMEM)
    tile = grads.shape[1:]
    return pl.pallas_call(
        functools.partial(sum_kernel, bands, sectors, share),
        in_specs=[whole, whole],
        out_specs=[whole, whole],
        out_shape=[
            jax.ShapeDtypeStruct(back.shape, BF16),
            jax.ShapeDtypeStruct((2, half) + tile, BF16),
        ],
        scratch_shapes=[
            pltpu.VMEM((half,) + tile, BF16),
            pltpu.VMEM((half,) + tile, BF16),
            pltpu.VMEM((half // 4,) + tile, BF16),
            pltpu.VMEM((unit,) + tile, BF16),
            pltpu.VMEM((3, half // 4) + tile, BF16),
            pltpu.VMEM((3, unit) + tile, BF16),
            pltpu.VMEM((4, unit) + tile, BF16),
            pltpu.SemaphoreType.DMA((5, 3, 3)),
            pltpu.SemaphoreType.DMA((5, 3, 3)),
            pltpu.SemaphoreType.DMA((8,)),
            pltpu.SemaphoreType.DMA((8,)),
            pltpu.SemaphoreType.DMA((8,)),
        ],
        compiler_params=pltpu.CompilerParams(collective_id=1, has_side_effects=True),
    )(back, grads.reshape((2, half) + tile))


def close_kernel(scale, rows_ref, arrived_ref, part_ref, sums_ref, ngrad_ref, *outs):
    n = part_ref.shape[0]
    total = part_ref[...]
    for j in range(8):
        total += dot(picked(rows_ref[0, j : j + 1, :], n), arrived_ref[j])
    ngrad_ref[...] = total
    at = 0
    for out in outs:
        for i in range(out.shape[0] // 16):
            for j in range(out.shape[1] // 128):
                out[16 * i : 16 * i + 16, 128 * j : 128 * j + 128] = sums_ref[at].astype(F32) * scale
                at += 1


def close_call(scale, rows, arrived, part, sums):
    d = part.shape[1]
    whole = pl.BlockSpec(memory_space=pltpu.VMEM)
    outs = [part.shape, (3 * d, d), (d, d), (2 * d, d), (d, d)]
    return pl.pallas_call(
        functools.partial(close_kernel, scale),
        in_specs=[whole] * 4,
        out_specs=[whole] * 5,
        out_shape=[jax.ShapeDtypeStruct(shape, F32) for shape in outs],
        compiler_params=pltpu.CompilerParams(vmem_limit_bytes=32 * 1024 * 1024),
    )(rows, arrived, part, sums.reshape((-1,) + sums.shape[2:]))


def solution(mesh):
    bands, sectors = mesh.shape["band"], mesh.shape["sector"]

    def local(node, edge, slot, mask, rows, w_ein, b_e, w_eout, g_e, w_nin, b_n, w_nout, g_n, ncot, ecot):
        n, d = node.shape
        far = fetch_call(bands, sectors, node, rows)
        nnew, enew, egrad, part, back, grads = layer_call(
            node, far.reshape(-1, d), edge, slot, mask,
            w_ein, b_e, w_eout, g_e, w_nin, b_n, w_nout, g_n, ncot, ecot,
        )
        arrived, sums = sum_call(bands, sectors, back, grads)
        scale = float(bands * sectors * n * slot.shape[1]) ** (-0.5)
        outs = close_call(scale, rows, arrived, part, sums)
        return (nnew, enew, outs[0], egrad) + tuple(outs[1:])

    split = P(("band", "sector"), None)
    in_specs = (split,) * 4 + (P(("band", "sector"), None, None),) + (P(),) * 8 + (split, split)
    out_specs = (split,) * 4 + (P(),) * 4
    return jax.shard_map(local, mesh=mesh, in_specs=in_specs, out_specs=out_specs, check_vma=False)
```

```python
import functools
import jax
import jax.numpy as jnp
from jax import lax
from jax.experimental import pallas as pl
from jax.experimental.pallas import tpu as pltpu
from jax.sharding import PartitionSpec as P

F32, BF16 = jnp.float32, jnp.bfloat16
R = 64
SUB = 2
D = 256


def dot(a, b):
    return jnp.dot(a, b, preferred_element_type=F32)


def dot_rows(a, b):
    return lax.dot_general(a, b, (((0,), (0,)), ((), ())), preferred_element_type=F32)


def silu_parts(pre):
    gate = 0.5 * jnp.tanh(0.5 * pre) + 0.5
    hidden = pre * gate
    return hidden, gate + hidden * (1.0 - gate)


def centred(matrix):
    return matrix - jnp.mean(matrix, 1, keepdims=True)


def flipped(matrix):
    return jnp.transpose(matrix.astype(F32)).astype(BF16)


band_steps = (-1, -1, -1, 0, 0, 1, 1, 1)
sector_steps = (-1, 0, 1, -1, 1, -1, 0, 1)
MESH = pl.DeviceIdType.MESH


def neighbours(bands, sectors):
    band, sector = lax.axis_index("band"), lax.axis_index("sector")
    ahead = [
        (lax.rem(band + b + bands, bands), lax.rem(sector + s + sectors, sectors))
        for b, s in zip(band_steps, sector_steps)
    ]
    return ahead


def partners(bands, sectors):
    band, sector = lax.axis_index("band"), lax.axis_index("sector")
    core = lax.rem(band, 2)
    x = lax.rem(band // 2, 4)
    z = band // 8
    places = [((z * 4 + lax.rem(x + i, 4)) * 2 + core, sector) for i in (1, 2, 3)]
    places += [((lax.rem(z + i, 4) * 4 + x) * 2 + core, sector) for i in (1, 2, 3)]
    return places + [(band, lax.rem(sector + 2, 4))]


def picked(wanted, count):
    line = lax.broadcasted_iota(jnp.int32, (count, wanted.shape[1]), 0)
    return jnp.where(line == wanted, 1.0, 0.0).astype(BF16)


def sum_over(
    bands, sectors, share, back_ref, grads_ref, arrived_ref, out_ref,
    half_ref, one_ref, two_ref, three_ref, first_in, second_in, third_in,
    send_sem, recv_sem, core_sem, back_send, back_recv,
):
    ahead = neighbours(bands, sectors)
    band, sector = lax.axis_index("band"), lax.axis_index("sector")
    core = lax.rem(band, 2)
    x = lax.rem(band // 2, 4)
    z = band // 8
    at = {"x": x, "y": sector, "z": z}

    def place(axis, index):
        if axis == "x":
            return ((z * 4 + index) * 2 + core, sector)
        if axis == "z":
            return ((index * 4 + x) * 2 + core, sector)
        return (band, index)

    def others(axis):
        return [lax.rem(at[axis] + i, 4) for i in (1, 2, 3)]

    sibling = (band + 1 - 2 * core, sector)
    returns = []
    core_copy = pltpu.make_async_remote_copy(
        src_ref=grads_ref.at[1 - core], dst_ref=half_ref,
        send_sem=core_sem.at[0], recv_sem=core_sem.at[1],
        device_id=sibling, device_id_type=MESH,
    )
    core_copy.start()
    for j in range(8):
        returns.append(
            pltpu.make_async_remote_copy(
                src_ref=back_ref.at[j], dst_ref=arrived_ref.at[j],
                send_sem=back_send.at[j], recv_sem=back_recv.at[j],
                device_id=ahead[j], device_id_type=MESH,
            )
        )
        returns[-1].start()

    orders = (("x", "y", "z"), ("y", "z", "x"), ("z", "x", "y"))
    starts = [16 * sum(share[:p]) for p in range(3)]

    def exchange(stage, p, axis, source, target):
        copies = []
        for i, other in enumerate(others(axis)):
            copies.append(
                pltpu.make_async_remote_copy(
                    src_ref=source(other, i), dst_ref=target(i),
                    send_sem=send_sem.at[stage, p, i], recv_sem=recv_sem.at[stage, p, i],
                    device_id=place(axis, other), device_id_type=MESH,
                )
            )
            copies[-1].start()
        return copies

    def finish(copies):
        for copy in copies:
            copy.wait()

    core_copy.wait()
    one_ref[...] = (grads_ref[core].astype(F32) + half_ref[...].astype(F32)).astype(BF16)

    live = []
    for p in range(3):
        m, axis = share[p], orders[p][0]
        live.append(exchange(
            0, p, axis,
            lambda other, i, p=p, m=m: one_ref.at[pl.ds(starts[p] + other * (4 * m), 4 * m)],
            lambda i, p=p, m=m: first_in.at[i, pl.ds(4 * sum(share[:p]), 4 * m)],
        ))
    for p in range(3):
        m, axis, low = share[p], orders[p][0], 4 * sum(share[:p])
        finish(live[p])
        total = one_ref[pl.ds(starts[p] + at[axis] * (4 * m), 4 * m)].astype(F32)
        for i in range(3):
            total += first_in[i, low : low + 4 * m].astype(F32)
        two_ref[low : low + 4 * m] = total.astype(BF16)
        live[p] = exchange(
            1, p, orders[p][1],
            lambda other, i, low=low, m=m: two_ref.at[pl.ds(low + other * m, m)],
            lambda i, p=p, m=m: second_in.at[i, pl.ds(sum(share[:p]), m)],
        )
    for p in range(3):
        m, axis, low, mid = share[p], orders[p][1], sum(share[:p]), 4 * sum(share[:p])
        finish(live[p])
        total = two_ref[pl.ds(mid + at[axis] * m, m)].astype(F32)
        for i in range(3):
            total += second_in[i, low : low + m].astype(F32)
        three_ref[low : low + m] = total.astype(BF16)
        third = orders[p][2]
        third_in[at[third], low : low + m] = total.astype(BF16)
        live[p] = exchange(
            2, p, third,
            lambda other, i, low=low, m=m: three_ref.at[pl.ds(low, m)],
            lambda i, low=low, m=m, third=third: third_in.at[at[third], pl.ds(low, m)],
        )
    for p in range(3):
        m, low = share[p], sum(share[:p])
        finish(live[p])
        total = third_in[0, low : low + m].astype(F32)
        for i in range(1, 4):
            total += third_in[i, low : low + m].astype(F32)
        spot = starts[p] + at[orders[p][0]] * (4 * m) + at[orders[p][1]] * m
        out_ref[core, pl.ds(spot, m)] = total.astype(BF16)
        live[p] = exchange(
            3, p, orders[p][1],
            lambda other, i, spot=spot, m=m: out_ref.at[core, pl.ds(spot, m)],
            lambda i, spot=spot, m=m: out_ref.at[core, pl.ds(spot, m)],
        )
    for p in range(3):
        m = share[p]
        finish(live[p])
        spot = starts[p] + at[orders[p][0]] * (4 * m)
        live[p] = exchange(
            4, p, orders[p][0],
            lambda other, i, spot=spot, m=m: out_ref.at[core, pl.ds(spot, 4 * m)],
            lambda i, spot=spot, m=m: out_ref.at[core, pl.ds(spot, 4 * m)],
        )
    last = []
    for p in range(3):
        finish(live[p])
        spot, m = starts[p], 16 * share[p]
        last.append(pltpu.make_async_remote_copy(
            src_ref=out_ref.at[core, pl.ds(spot, m)], dst_ref=out_ref.at[core, pl.ds(spot, m)],
            send_sem=core_sem.at[2 + p], recv_sem=core_sem.at[5 + p],
            device_id=sibling, device_id_type=MESH,
        ))
        last[-1].start()
    finish(returns)
    finish(last)


def layer_kernel(
    bands, sectors, steps, slots, scale, share,
    own_ref, rows_ref, edge_ref, slot_ref, mask_ref,
    w_ein, b_e, w_eout, g_e, w_nin, b_n, w_nout, g_n, ncot_ref, ecot_ref,
    nnew_ref, enew_ref, egrad_ref, ngrad_ref, gein_ref, geout_ref, gnin_ref, gnout_ref,
    x_ref, xt_ref, g_ref, dz_ref, dpre_ref, wcat_ref, weo_ref, weot_ref, wet_ref, recv_ref, parts_ref, partst_ref,
    column_ref, line_ref, hid_ref, dsil_ref, xh_ref, rm_ref, gath_ref, dgath_ref,
    acc_ref, gout_ref, gd_ref, down_ref, gnode_ref,
    far_ref, out_ref, back_ref, arrived_ref, grads_ref, sums_ref,
    half_ref, one_ref, two_ref, three_ref, first_in, second_in, third_in,
    fetch_send, fetch_recv, send_sem, recv_sem, core_sem, back_send, back_recv,
):
    t = pl.program_id(0)
    rows = R * slots
    n = own_ref.shape[0]
    table = n + far_ref.shape[0] * far_ref.shape[1]
    seg = D + table

    tile_rows = slots * R

    def spread_rows(ref, base):
        upper = lax.broadcasted_iota(jnp.int32, (8, ref.shape[1]), 0) < 4
        pieces = []
        for pair in range(R // 2):
            a = jnp.broadcast_to(ref[pl.ds(base + 2 * pair, 1), :], (8, ref.shape[1]))
            b = jnp.broadcast_to(ref[pl.ds(base + 2 * pair + 1, 1), :], (8, ref.shape[1]))
            pieces += [a, jnp.where(upper, a, b), b]
        return jnp.concatenate(pieces, axis=0)

    @pl.when(t == 0)
    def _():
        ahead = neighbours(bands, sectors)
        barrier = pltpu.get_barrier_semaphore()
        everyone = ahead + partners(bands, sectors)
        for place in everyone:
            pl.semaphore_signal(barrier, inc=1, device_id=place, device_id_type=MESH)
        node = own_ref[...]
        for j in range(8):
            choice = picked(rows_ref[0, j : j + 1, :], n)
            out_ref[j] = dot_rows(choice, node).astype(BF16)
        pl.semaphore_wait(barrier, len(everyone))
        copies = []
        for j in range(8):
            copies.append(
                pltpu.make_async_remote_copy(
                    src_ref=out_ref.at[j], dst_ref=far_ref.at[j],
                    send_sem=fetch_send.at[j], recv_sem=fetch_recv.at[j],
                    device_id=ahead[7 - j], device_id_type=MESH,
                )
            )
            copies[-1].start()
        e = lax.broadcasted_iota(jnp.int32, (R, rows), 1)
        r = lax.broadcasted_iota(jnp.int32, (R, rows), 0)
        gap = e - slots * r
        inside = (gap >= 0) & (gap < slots)
        g_ref[...] = jnp.where(inside, 1.0, 0.0).astype(BF16)
        ef = lax.broadcasted_iota(jnp.int32, (32, rows), 1).astype(F32)
        lf = lax.broadcasted_iota(jnp.int32, (32, rows), 0).astype(F32)
        k = ef - slots * jnp.floor((ef + 0.5) * (1.0 / slots))
        selt = jnp.where(lf == k, 32.0, 0.0) + jnp.where(lf == k + 16.0, 1.0, 0.0)
        ef = lax.broadcasted_iota(jnp.int32, (rows, 128), 0).astype(F32)
        lf = lax.broadcasted_iota(jnp.int32, (rows, 128), 1).astype(F32)
        k = ef - slots * jnp.floor((ef + 0.5) * (1.0 / slots))
        sel = jnp.where(lf == k, 1.0, 0.0)
        v = slot_ref[...] + 1024 * mask_ref[...]
        partst_ref[...] = jnp.zeros_like(partst_ref)
        partst_ref[0:slots, :] = (v >> 5).astype(F32)
        partst_ref[16 : 16 + slots, :] = (v & 31).astype(F32)
        parts = jnp.transpose(partst_ref[...])
        parts_ref[...] = parts.astype(BF16)
        partst_ref[0:slots, :] = v.astype(F32)
        down_ref[:, 0:128] = jnp.transpose(partst_ref[...])
        for tile in range(n // R):
            piece = dot_rows(parts_ref[tile * R : tile * R + R, 0:32], g_ref[...])
            line_ref[tile] = jnp.sum(piece * selt, 0, keepdims=True)
            spread = spread_rows(down_ref.at[:, 0:128], tile * R)
            column_ref[tile * rows : tile * rows + rows, :] = jnp.sum(spread * sel, 1, keepdims=True)
        wcat_ref[0:D, :] = w_ein[0:D, :]
        wcat_ref[D : D + n, :] = dot(own_ref[...], w_ein[D : 2 * D, :]).astype(BF16)
        recv_ref[...] = dot(own_ref[...], w_ein[2 * D :, :]) + b_e[...]
        weo = centred(w_eout[...].astype(F32))
        weo_ref[...] = weo.astype(BF16)
        weot_ref[...] = jnp.transpose(weo).astype(BF16)
        wet_ref[...] = flipped(w_ein[0:D, :])
        acc_ref[...] = jnp.zeros_like(acc_ref)
        gout_ref[...] = jnp.zeros_like(gout_ref)
        for copy in copies:
            copy.wait()
        far = far_ref[...].reshape(table - n, D)
        wcat_ref[D + n : seg, :] = dot(far, w_ein[D : 2 * D, :]).astype(BF16)

    def spots(step, s):
        at = step * (R * SUB) + s * R
        here = pl.ds(pl.multiple_of(at * slots, rows), rows)
        mine = pl.ds(pl.multiple_of(at, R), R)
        return here, mine, slice(s * rows, (s + 1) * rows)

    def first_half(s):
        here, mine, part = spots(t, s)
        x = x_ref.at[s]
        x[:, 0:D] = edge_ref[part, :]
        v = column_ref[here, :]
        real = v >= 1024.0
        slot = jnp.where(real, v - 1024.0, v)
        lane = lax.broadcasted_iota(jnp.int32, (rows, D), 1).astype(F32).astype(BF16)
        for block in range(table // D):
            wanted = (slot - float(block * D)).astype(BF16)
            x[:, D + block * D : 2 * D + block * D] = jnp.where(
                lane == wanted, jnp.ones((), BF16), jnp.zeros((), BF16)
            )
        base = pl.multiple_of(t * (R * SUB) + s * R, R)
        pre = dot(x[...], wcat_ref[...]) + spread_rows(recv_ref, base)
        return pre, jnp.where(real, 1.0, 0.0)

    def second_half(s, pre, keep):
        here, mine, part = spots(t, s)
        hidden, slope = silu_parts(pre)
        hidden = hidden.astype(BF16)
        hid_ref[here, :] = hidden
        dsil_ref[here, :] = slope.astype(BF16)
        c = dot(hidden, weo_ref[...])
        rstd = lax.rsqrt(jnp.mean(c * c, 1, keepdims=True) + 1e-05)
        normed = c * rstd
        xh_ref[here, :] = normed.astype(BF16)
        rm_ref[here, :] = rstd * keep
        update = normed * g_e[...] * keep
        enew_ref[part, :] = (edge_ref[part, :].astype(F32) + update).astype(BF16)
        gath_ref[mine, :] = dot(g_ref[...], update.astype(BF16)).astype(BF16)

    @pl.when(t < steps)
    def _():
        held = first_half(0)
        for s in range(1, SUB):
            following = first_half(s)
            second_half(s - 1, *held)
            held = following
        second_half(SUB - 1, *held)

    @pl.when(t == steps)
    def _():
        own = own_ref[...]
        gath = gath_ref[...]
        pre = dot(own, w_nin[0:D, :]) + dot(gath, w_nin[D:, :]) + b_n[...]
        hidden, slope = silu_parts(pre)
        hidden = hidden.astype(BF16)
        wno = centred(w_nout[...].astype(F32))
        c = dot(hidden, wno.astype(BF16))
        rstd = lax.rsqrt(jnp.mean(c * c, 1, keepdims=True) + 1e-05)
        normed = c * rstd
        nnew_ref[...] = (own.astype(F32) + normed * g_n[...]).astype(BF16)
        cot = ncot_ref[...].astype(F32)
        dx = cot * g_n[...]
        share = jnp.mean(dx * normed, 1, keepdims=True)
        dz = (rstd * (dx - normed * share)).astype(BF16)
        gnode_ref[2 * D : 3 * D, :] = centred(dot_rows(hidden, dz))
        dpre = (dot(dz, jnp.transpose(wno).astype(BF16)) * slope).astype(BF16)
        gnode_ref[0:D, :] = dot_rows(own, dpre)
        gnode_ref[D : 2 * D, :] = dot_rows(gath, dpre)
        down_ref[...] = cot + dot(dpre, flipped(w_nin[0:D, :]))
        dgath_ref[...] = dot(dpre, flipped(w_nin[D:, :]))

    def third_half(s):
        here, mine, part = spots(t - steps - 1, s)
        v = line_ref[(t - steps - 1) * SUB + s]
        slot = jnp.where(v >= 1024.0, v - 1024.0, v)
        xt_ref[0:D, part] = jnp.transpose(edge_ref[part, :])
        line = lax.broadcasted_iota(jnp.int32, (D, rows), 0).astype(F32).astype(BF16)
        for block in range(table // D):
            wanted = (slot - float(block * D)).astype(BF16)
            xt_ref[D + block * D : 2 * D + block * D, part] = jnp.where(
                line == wanted, jnp.ones((), BF16), jnp.zeros((), BF16)
            )
        cot = ecot_ref[part, :].astype(F32)
        base = pl.multiple_of((t - steps - 1) * (R * SUB) + s * R, R)
        dx = (cot + spread_rows(dgath_ref, base)) * g_e[...]
        normed = xh_ref[here, :].astype(F32)
        share_of = jnp.mean(dx * normed, 1, keepdims=True)
        dz = (rm_ref[here, :] * (dx - normed * share_of)).astype(BF16)
        dz_ref[part, :] = dz
        dpre = (dot(dz, weot_ref[...]) * dsil_ref[here, :].astype(F32)).astype(BF16)
        dpre_ref[part, :] = dpre
        egrad_ref[part, :] = (cot + dot(dpre, wet_ref[...])).astype(BF16)
        gd_ref[mine, :] = dot(g_ref[...], dpre).astype(BF16)

    @pl.when(t > steps)
    def _():
        for s in range(SUB):
            third_half(s)
        span = pl.ds(pl.multiple_of((t - steps - 1) * (rows * SUB), rows), rows * SUB)
        gout_ref[...] += dot_rows(hid_ref[span, :], dz_ref[...])
        acc_ref[...] += dot(xt_ref[...], dpre_ref[...])

    @pl.when(t == 2 * steps)
    def _():
        own = own_ref[...]
        near = acc_ref[D : D + n, :].astype(BF16)
        far = acc_ref[D + n : seg, :].astype(BF16)
        wst = flipped(w_ein[D : 2 * D, :])
        back_ref[...] = dot(far, wst).astype(BF16).reshape(back_ref.shape)
        gd = gd_ref[...]
        down_ref[...] += dot(near, wst) + dot(gd, flipped(w_ein[2 * D :, :]))
        g_s = dot_rows(own, near) + dot_rows(far_ref[...].reshape(table - n, D), far)
        g_r = dot_rows(own, gd)
        whole = [acc_ref[0:D, :], g_s, g_r, centred(gout_ref[...])]
        whole += [gnode_ref[i * D : (i + 1) * D, :] for i in range(3)]
        at = 0
        for piece in whole:
            for i in range(D // 16):
                for j in range(2):
                    grads_ref[at // 112, at % 112] = piece[16 * i : 16 * i + 16, 128 * j : 128 * j + 128].astype(BF16)
                    at += 1
        sum_over(
            bands, sectors, share, back_ref, grads_ref, arrived_ref, sums_ref,
            half_ref, one_ref, two_ref, three_ref, first_in, second_in, third_in,
            send_sem, recv_sem, core_sem, back_send, back_recv,
        )
        total = down_ref[...]
        for j in range(8):
            total += dot(picked(rows_ref[0, j : j + 1, :], n), arrived_ref[j])
        ngrad_ref[...] = total
        at = 0
        for out in (gein_ref, geout_ref, gnin_ref, gnout_ref):
            for i in range(out.shape[0] // 16):
                for j in range(2):
                    out[16 * i : 16 * i + 16, 128 * j : 128 * j + 128] = sums_ref[at // 112, at % 112].astype(F32) * scale
                    at += 1


def layer_call(bands, sectors, node, rows_in, edge, slot, mask, w_ein, b_e, w_eout, g_e, w_nin, b_n, w_nout, g_n, ncot, ecot):
    n, d = node.shape
    slots = slot.shape[1]
    rows = R * slots
    tiles = n // (R * SUB)
    cap = rows_in.shape[2]
    table = n + 8 * cap
    unit = 7
    share = (3, 2, 2)
    scale = float(bands * sectors * n * slots) ** (-0.5)
    half = 16 * unit
    tile = (16, 128)
    seg = d + table
    total = n * slots
    whole = pl.BlockSpec(memory_space=pltpu.VMEM)
    stream_e = pl.BlockSpec((rows * SUB, d), lambda t: (jnp.where(t < tiles, t, jnp.maximum(t - tiles - 1, 0)), 0))
    first = pl.BlockSpec((rows * SUB, d), lambda t: (jnp.minimum(t, tiles - 1), 0))
    second = pl.BlockSpec((rows * SUB, d), lambda t: (jnp.maximum(t - tiles - 1, 0), 0))
    tiles_all = 7 * (d // 16) * (d // 128)
    flops = 2 * total * d * (d * 8 + 2 * table)
    return pl.pallas_call(
        functools.partial(layer_kernel, bands, sectors, tiles, slots, scale, share),
        grid=(2 * tiles + 1,),
        in_specs=[whole, whole, stream_e] + [whole] * 11 + [second],
        out_specs=[whole, first, second] + [whole] * 5,
        out_shape=[
            jax.ShapeDtypeStruct((n, d), BF16),
            jax.ShapeDtypeStruct((total, d), BF16),
            jax.ShapeDtypeStruct((total, d), BF16),
            jax.ShapeDtypeStruct((n, d), F32),
            jax.ShapeDtypeStruct((3 * d, d), F32),
            jax.ShapeDtypeStruct((d, d), F32),
            jax.ShapeDtypeStruct((2 * d, d), F32),
            jax.ShapeDtypeStruct((d, d), F32),
        ],
        scratch_shapes=[
            pltpu.VMEM((SUB, rows, seg), BF16),
            pltpu.VMEM((seg, SUB * rows), BF16),
            pltpu.VMEM((R, rows), BF16),
            pltpu.VMEM((SUB * rows, d), BF16),
            pltpu.VMEM((SUB * rows, d), BF16),
            pltpu.VMEM((seg, d), BF16),
            pltpu.VMEM((d, d), BF16),
            pltpu.VMEM((d, d), BF16),
            pltpu.VMEM((d, d), BF16),
            pltpu.VMEM((n, d), F32),
            pltpu.VMEM((n, 128), BF16),
            pltpu.VMEM((128, n), F32),
            pltpu.VMEM((total, 1), F32),
            pltpu.VMEM((n // R, 1, rows), F32),
            pltpu.VMEM((total, d), BF16),
            pltpu.VMEM((total, d), BF16),
            pltpu.VMEM((total, d), BF16),
            pltpu.VMEM((total, 1), F32),
            pltpu.VMEM((n, d), BF16),
            pltpu.VMEM((n, d), F32),
            pltpu.VMEM((seg, d), F32),
            pltpu.VMEM((d, d), F32),
            pltpu.VMEM((n, d), BF16),
            pltpu.VMEM((n, d), F32),
            pltpu.VMEM((3 * d, d), F32),
            pltpu.VMEM((8, cap, d), BF16),
            pltpu.VMEM((8, cap, d), BF16),
            pltpu.VMEM((8, cap, d), BF16),
            pltpu.VMEM((8, cap, d), BF16),
            pltpu.VMEM((2, half) + tile, BF16),
            pltpu.VMEM((2, half) + tile, BF16),
            pltpu.VMEM((half,) + tile, BF16),
            pltpu.VMEM((half,) + tile, BF16),
            pltpu.VMEM((half // 4,) + tile, BF16),
            pltpu.VMEM((unit,) + tile, BF16),
            pltpu.VMEM((3, half // 4) + tile, BF16),
            pltpu.VMEM((3, unit) + tile, BF16),
            pltpu.VMEM((4, unit) + tile, BF16),
            pltpu.SemaphoreType.DMA((8,)),
            pltpu.SemaphoreType.DMA((8,)),
            pltpu.SemaphoreType.DMA((5, 3, 3)),
            pltpu.SemaphoreType.DMA((5, 3, 3)),
            pltpu.SemaphoreType.DMA((8,)),
            pltpu.SemaphoreType.DMA((8,)),
            pltpu.SemaphoreType.DMA((8,)),
        ],
        compiler_params=pltpu.CompilerParams(
            vmem_limit_bytes=60 * 1024 * 1024, collective_id=0, has_side_effects=True
        ),
        cost_estimate=pl.CostEstimate(flops=flops, bytes_accessed=5 * total * d * 2, transcendentals=total * d),
    )(node, rows_in, edge, slot.T, mask.T, w_ein, b_e.reshape(1, -1), w_eout, g_e.reshape(1, -1), w_nin, b_n.reshape(1, -1), w_nout, g_n.reshape(1, -1), ncot, ecot)


def solution(mesh):
    bands, sectors = mesh.shape["band"], mesh.shape["sector"]

    def local(node, edge, slot, mask, rows, w_ein, b_e, w_eout, g_e, w_nin, b_n, w_nout, g_n, ncot, ecot):
        nnew, enew, egrad, ngrad, gein, geout, gnin, gnout = layer_call(
            bands, sectors, node, rows, edge, slot, mask,
            w_ein, b_e, w_eout, g_e, w_nin, b_n, w_nout, g_n, ncot, ecot,
        )
        return nnew, enew, ngrad, egrad, gein, geout, gnin, gnout

    split = P(("band", "sector"), None)
    in_specs = (split,) * 4 + (P(("band", "sector"), None, None),) + (P(),) * 8 + (split, split)
    out_specs = (split,) * 4 + (P(),) * 4
    return jax.shard_map(local, mesh=mesh, in_specs=in_specs, out_specs=out_specs, check_vma=False)
```

```python
import functools
import jax
import jax.numpy as jnp
from jax import lax
from jax.experimental import pallas as pl
from jax.experimental.pallas import tpu as pltpu
from jax.sharding import PartitionSpec as P

F32, BF16 = jnp.float32, jnp.bfloat16
R = 64
SUB = 4
D = 256


def dot(a, b):
    return jnp.dot(a, b, preferred_element_type=F32)


def dot_rows(a, b):
    return lax.dot_general(a, b, (((0,), (0,)), ((), ())), preferred_element_type=F32)


def silu_parts(pre):
    gate = 0.5 * jnp.tanh(0.5 * pre) + 0.5
    hidden = pre * gate
    return hidden, gate + hidden * (1.0 - gate)


def centred(matrix):
    return matrix - jnp.mean(matrix, 1, keepdims=True)


def flipped(matrix):
    return jnp.transpose(matrix.astype(F32)).astype(BF16)


def layer_kernel(
    steps, slots,
    own_ref, far_ref, edge_ref, slot_ref, mask_ref,
    w_ein, b_e, w_eout, g_e, w_nin, b_n, w_nout, g_n, ncot_ref, ecot_ref,
    nnew_ref, enew_ref, egrad_ref, ngrad_ref, back_ref, grads_ref,
    x_ref, xt_ref, g_ref, dz_ref, dpre_ref, wcat_ref, weo_ref, weot_ref, wet_ref, recv_ref, value_ref, parts_ref, partst_ref,
    sel_ref, line_ref, hid_ref, dsil_ref, xh_ref, rm_ref, gath_ref, dgath_ref,
    acc_ref, gout_ref, gd_ref, down_ref, gnode_ref,
):
    t = pl.program_id(0)
    rows = R * slots
    n = own_ref.shape[0]
    table = n + far_ref.shape[0]
    seg = D + table

    def spread_rows(ref, base):
        upper = lax.broadcasted_iota(jnp.int32, (8, ref.shape[1]), 0) < 4
        pieces = []
        for pair in range(R // 2):
            a = jnp.broadcast_to(ref[pl.ds(base + 2 * pair, 1), :], (8, ref.shape[1]))
            b = jnp.broadcast_to(ref[pl.ds(base + 2 * pair + 1, 1), :], (8, ref.shape[1]))
            pieces += [a, jnp.where(upper, a, b), b]
        return jnp.concatenate(pieces, axis=0)

    @pl.when(t == 0)
    def _():
        e = lax.broadcasted_iota(jnp.int32, (R, rows), 1)
        r = lax.broadcasted_iota(jnp.int32, (R, rows), 0)
        gap = e - slots * r
        inside = (gap >= 0) & (gap < slots)
        g_ref[...] = jnp.where(inside, 1.0, 0.0).astype(BF16)
        ef = lax.broadcasted_iota(jnp.int32, (32, rows), 1).astype(F32)
        lf = lax.broadcasted_iota(jnp.int32, (32, rows), 0).astype(F32)
        k = ef - slots * jnp.floor((ef + 0.5) * (1.0 / slots))
        selt = jnp.where(lf == k, 32.0, 0.0) + jnp.where(lf == k + 16.0, 1.0, 0.0)
        ef = lax.broadcasted_iota(jnp.int32, (rows, 128), 0).astype(F32)
        lf = lax.broadcasted_iota(jnp.int32, (rows, 128), 1).astype(F32)
        k = ef - slots * jnp.floor((ef + 0.5) * (1.0 / slots))
        sel_ref[...] = jnp.where(lf == k, 1.0, 0.0)
        v = slot_ref[...] + 1024 * mask_ref[...]
        partst_ref[...] = jnp.zeros_like(partst_ref)
        partst_ref[0:slots, :] = v.astype(F32)
        value_ref[...] = jnp.transpose(partst_ref[...])
        high = (v >> 5).astype(F32)
        low = (v & 31).astype(F32)
        parts_ref[...] = jnp.zeros_like(parts_ref)
        parts_ref[0:16, :] = jnp.concatenate([high, jnp.zeros((16 - slots, n), F32)], axis=0).astype(BF16)
        parts_ref[16:32, :] = jnp.concatenate([low, jnp.zeros((16 - slots, n), F32)], axis=0).astype(BF16)
        for tile in range(n // R):
            piece = dot(parts_ref[0:32, tile * R : tile * R + R], g_ref[...])
            line_ref[tile] = jnp.sum(piece * selt, 0, keepdims=True)
        wcat_ref[0:D, :] = w_ein[0:D, :]
        wcat_ref[D : D + n, :] = dot(own_ref[...], w_ein[D : 2 * D, :]).astype(BF16)
        wcat_ref[D + n : seg, :] = dot(far_ref[...], w_ein[D : 2 * D, :]).astype(BF16)
        recv_ref[...] = dot(own_ref[...], w_ein[2 * D :, :]) + b_e[...]
        weo = centred(w_eout[...].astype(F32))
        weo_ref[...] = weo.astype(BF16)
        weot_ref[...] = jnp.transpose(weo).astype(BF16)
        wet_ref[...] = flipped(w_ein[0:D, :])
        acc_ref[...] = jnp.zeros_like(acc_ref)
        gout_ref[...] = jnp.zeros_like(gout_ref)

    def spots(step, s):
        at = step * (R * SUB) + s * R
        here = pl.ds(pl.multiple_of(at * slots, rows), rows)
        mine = pl.ds(pl.multiple_of(at, R), R)
        return here, mine, slice(s * rows, (s + 1) * rows)

    def first_half(s):
        here, mine, part = spots(t, s)
        x = x_ref.at[s]
        x[:, 0:D] = edge_ref[part, :]
        base = pl.multiple_of(t * (R * SUB) + s * R, R)
        v = jnp.sum(spread_rows(value_ref, base) * sel_ref[...], 1, keepdims=True)
        real = v >= 1024.0
        slot = jnp.where(real, v - 1024.0, v)
        lane = lax.broadcasted_iota(jnp.int32, (rows, D), 1).astype(F32).astype(BF16)
        for block in range(table // D):
            wanted = (slot - float(block * D)).astype(BF16)
            x[:, D + block * D : 2 * D + block * D] = jnp.where(
                lane == wanted, jnp.ones((), BF16), jnp.zeros((), BF16)
            )
        pre = dot(x[...], wcat_ref[...]) + spread_rows(recv_ref, base)
        return pre, jnp.where(real, 1.0, 0.0)

    def second_half(s, pre, keep):
        here, mine, part = spots(t, s)
        hidden, slope = silu_parts(pre)
        hidden = hidden.astype(BF16)
        hid_ref[here, :] = hidden
        dsil_ref[here, :] = slope.astype(BF16)
        c = dot(hidden, weo_ref[...])
        rstd = lax.rsqrt(jnp.mean(c * c, 1, keepdims=True) + 1e-05)
        normed = c * rstd
        xh_ref[here, :] = normed.astype(BF16)
        rm_ref[here, :] = rstd * keep
        update = normed * g_e[...] * keep
        enew_ref[part, :] = (edge_ref[part, :].astype(F32) + update).astype(BF16)
        gath_ref[mine, :] = dot(g_ref[...], update.astype(BF16)).astype(BF16)

    @pl.when(t < steps)
    def _():
        held = first_half(0)
        for s in range(1, SUB):
            following = first_half(s)
            second_half(s - 1, *held)
            held = following
        second_half(SUB - 1, *held)

    @pl.when(t == steps)
    def _():
        own = own_ref[...]
        gath = gath_ref[...]
        pre = dot(own, w_nin[0:D, :]) + dot(gath, w_nin[D:, :]) + b_n[...]
        hidden, slope = silu_parts(pre)
        hidden = hidden.astype(BF16)
        wno = centred(w_nout[...].astype(F32))
        c = dot(hidden, wno.astype(BF16))
        rstd = lax.rsqrt(jnp.mean(c * c, 1, keepdims=True) + 1e-05)
        normed = c * rstd
        nnew_ref[...] = (own.astype(F32) + normed * g_n[...]).astype(BF16)
        cot = ncot_ref[...].astype(F32)
        dx = cot * g_n[...]
        share = jnp.mean(dx * normed, 1, keepdims=True)
        dz = (rstd * (dx - normed * share)).astype(BF16)
        gnode_ref[2 * D : 3 * D, :] = centred(dot_rows(hidden, dz))
        dpre = (dot(dz, jnp.transpose(wno).astype(BF16)) * slope).astype(BF16)
        gnode_ref[0:D, :] = dot_rows(own, dpre)
        gnode_ref[D : 2 * D, :] = dot_rows(gath, dpre)
        down_ref[...] = cot + dot(dpre, flipped(w_nin[0:D, :]))
        dgath_ref[...] = dot(dpre, flipped(w_nin[D:, :]))

    def third_half(s):
        here, mine, part = spots(t - steps - 1, s)
        v = line_ref[(t - steps - 1) * SUB + s]
        slot = jnp.where(v >= 1024.0, v - 1024.0, v)
        xt_ref[0:D, part] = jnp.transpose(edge_ref[part, :])
        line = lax.broadcasted_iota(jnp.int32, (D, rows), 0).astype(F32).astype(BF16)
        for block in range(table // D):
            wanted = (slot - float(block * D)).astype(BF16)
            xt_ref[D + block * D : 2 * D + block * D, part] = jnp.where(
                line == wanted, jnp.ones((), BF16), jnp.zeros((), BF16)
            )
        cot = ecot_ref[part, :].astype(F32)
        base = pl.multiple_of((t - steps - 1) * (R * SUB) + s * R, R)
        dx = (cot + spread_rows(dgath_ref, base)) * g_e[...]
        normed = xh_ref[here, :].astype(F32)
        share_of = jnp.mean(dx * normed, 1, keepdims=True)
        dz = (rm_ref[here, :] * (dx - normed * share_of)).astype(BF16)
        dz_ref[part, :] = dz
        dpre = (dot(dz, weot_ref[...]) * dsil_ref[here, :].astype(F32)).astype(BF16)
        dpre_ref[part, :] = dpre
        egrad_ref[part, :] = (cot + dot(dpre, wet_ref[...])).astype(BF16)
        gd_ref[mine, :] = dot(g_ref[...], dpre).astype(BF16)

    @pl.when(t > steps)
    def _():
        for s in range(SUB):
            third_half(s)
        span = pl.ds(pl.multiple_of((t - steps - 1) * (rows * SUB), rows), rows * SUB)
        gout_ref[...] += dot_rows(hid_ref[span, :], dz_ref[...])
        acc_ref[...] += dot(xt_ref[...], dpre_ref[...])

    @pl.when(t == 2 * steps)
    def _():
        own = own_ref[...]
        near = acc_ref[D : D + n, :].astype(BF16)
        far = acc_ref[D + n : seg, :].astype(BF16)
        wst = flipped(w_ein[D : 2 * D, :])
        back_ref[...] = dot(far, wst).astype(BF16).reshape(back_ref.shape)
        gd = gd_ref[...]
        ngrad_ref[...] = down_ref[...] + dot(near, wst) + dot(gd, flipped(w_ein[2 * D :, :]))
        g_s = dot_rows(own, near) + dot_rows(far_ref[...], far)
        g_r = dot_rows(own, gd)
        whole = [acc_ref[0:D, :], g_s, g_r, centred(gout_ref[...])]
        whole += [gnode_ref[i * D : (i + 1) * D, :] for i in range(3)]
        at = 0
        for piece in whole:
            for i in range(D // 16):
                for j in range(2):
                    grads_ref[at] = piece[16 * i : 16 * i + 16, 128 * j : 128 * j + 128].astype(BF16)
                    at += 1


def layer_call(node, far, edge, slot, mask, w_ein, b_e, w_eout, g_e, w_nin, b_n, w_nout, g_n, ncot, ecot):
    n, d = node.shape
    slots = slot.shape[1]
    rows = R * slots
    tiles = n // (R * SUB)
    table = n + far.shape[0]
    seg = d + table
    total = n * slots
    whole = pl.BlockSpec(memory_space=pltpu.VMEM)
    stream_e = pl.BlockSpec((rows * SUB, d), lambda t: (jnp.where(t < tiles, t, jnp.maximum(t - tiles - 1, 0)), 0))
    first = pl.BlockSpec((rows * SUB, d), lambda t: (jnp.minimum(t, tiles - 1), 0))
    second = pl.BlockSpec((rows * SUB, d), lambda t: (jnp.maximum(t - tiles - 1, 0), 0))
    tiles_all = 7 * (d // 16) * (d // 128)
    flops = 2 * total * d * (d * 8 + 2 * table)
    return pl.pallas_call(
        functools.partial(layer_kernel, tiles, slots),
        grid=(2 * tiles + 1,),
        in_specs=[whole, whole, stream_e] + [whole] * 11 + [second],
        out_specs=[whole, first, second, whole, whole, whole],
        out_shape=[
            jax.ShapeDtypeStruct((n, d), BF16),
            jax.ShapeDtypeStruct((total, d), BF16),
            jax.ShapeDtypeStruct((total, d), BF16),
            jax.ShapeDtypeStruct((n, d), F32),
            jax.ShapeDtypeStruct((8, far.shape[0] // 8, d), BF16),
            jax.ShapeDtypeStruct((tiles_all, 16, 128), BF16),
        ],
        scratch_shapes=[
            pltpu.VMEM((SUB, rows, seg), BF16),
            pltpu.VMEM((seg, SUB * rows), BF16),
            pltpu.VMEM((R, rows), BF16),
            pltpu.VMEM((SUB * rows, d), BF16),
            pltpu.VMEM((SUB * rows, d), BF16),
            pltpu.VMEM((seg, d), BF16),
            pltpu.VMEM((d, d), BF16),
            pltpu.VMEM((d, d), BF16),
            pltpu.VMEM((d, d), BF16),
            pltpu.VMEM((n, d), F32),
            pltpu.VMEM((n, 128), F32),
            pltpu.VMEM((32, n), BF16),
            pltpu.VMEM((128, n), F32),
            pltpu.VMEM((rows, 128), F32),
            pltpu.VMEM((n // R, 1, rows), F32),
            pltpu.VMEM((total, d), BF16),
            pltpu.VMEM((total, d), BF16),
            pltpu.VMEM((total, d), BF16),
            pltpu.VMEM((total, 1), F32),
            pltpu.VMEM((n, d), BF16),
            pltpu.VMEM((n, d), F32),
            pltpu.VMEM((seg, d), F32),
            pltpu.VMEM((d, d), F32),
            pltpu.VMEM((n, d), BF16),
            pltpu.VMEM((n, d), F32),
            pltpu.VMEM((3 * d, d), F32),
        ],
        compiler_params=pltpu.CompilerParams(vmem_limit_bytes=60 * 1024 * 1024),
        cost_estimate=pl.CostEstimate(flops=flops, bytes_accessed=5 * total * d * 2, transcendentals=total * d),
    )(node, far, edge, slot.T, mask.T, w_ein, b_e.reshape(1, -1), w_eout, g_e.reshape(1, -1), w_nin, b_n.reshape(1, -1), w_nout, g_n.reshape(1, -1), ncot, ecot)


band_steps = (-1, -1, -1, 0, 0, 1, 1, 1)
sector_steps = (-1, 0, 1, -1, 1, -1, 0, 1)
MESH = pl.DeviceIdType.MESH


def neighbours(bands, sectors):
    band, sector = lax.axis_index("band"), lax.axis_index("sector")
    ahead = [
        (lax.rem(band + b + bands, bands), lax.rem(sector + s + sectors, sectors))
        for b, s in zip(band_steps, sector_steps)
    ]
    return ahead


def picked(wanted, count):
    line = lax.broadcasted_iota(jnp.int32, (count, wanted.shape[1]), 0)
    return jnp.where(line == wanted, 1.0, 0.0).astype(BF16)


def fetch_kernel(bands, sectors, node_ref, rows_ref, far_ref, out_ref, send_sem, recv_sem):
    ahead = neighbours(bands, sectors)
    barrier = pltpu.get_barrier_semaphore()
    for place in ahead:
        pl.semaphore_signal(barrier, inc=1, device_id=place, device_id_type=MESH)
    node = node_ref[...]
    for j in range(8):
        choice = picked(rows_ref[0, j : j + 1, :], node.shape[0])
        out_ref[j] = dot_rows(choice, node).astype(BF16)
    pl.semaphore_wait(barrier, 8)
    copies = []
    for j in range(8):
        copies.append(
            pltpu.make_async_remote_copy(
                src_ref=out_ref.at[j],
                dst_ref=far_ref.at[j],
                send_sem=send_sem.at[j],
                recv_sem=recv_sem.at[j],
                device_id=ahead[7 - j],
                device_id_type=MESH,
            )
        )
        copies[-1].start()
    for copy in copies:
        copy.wait()


def fetch_call(bands, sectors, node, rows):
    cap, d = rows.shape[2], node.shape[1]
    whole = pl.BlockSpec(memory_space=pltpu.VMEM)
    return pl.pallas_call(
        functools.partial(fetch_kernel, bands, sectors),
        in_specs=[whole, whole],
        out_specs=whole,
        out_shape=jax.ShapeDtypeStruct((8, cap, d), BF16),
        scratch_shapes=[
            pltpu.VMEM((8, cap, d), BF16),
            pltpu.SemaphoreType.DMA((8,)),
            pltpu.SemaphoreType.DMA((8,)),
        ],
        compiler_params=pltpu.CompilerParams(
            collective_id=0, has_side_effects=True, vmem_limit_bytes=60 * 1024 * 1024
        ),
    )(node, rows)


def sum_kernel(
    bands, sectors, share, back_ref, grads_ref, arrived_ref, out_ref,
    half_ref, one_ref, two_ref, three_ref, first_in, second_in, third_in,
    mine_ref, send_sem, recv_sem, core_sem, back_send, back_recv, load_sem,
):
    ahead = neighbours(bands, sectors)
    band, sector = lax.axis_index("band"), lax.axis_index("sector")
    core = lax.rem(band, 2)
    x = lax.rem(band // 2, 4)
    z = band // 8
    at = {"x": x, "y": sector, "z": z}

    def place(axis, index):
        if axis == "x":
            return ((z * 4 + index) * 2 + core, sector)
        if axis == "z":
            return ((index * 4 + x) * 2 + core, sector)
        return (band, index)

    def others(axis):
        return [lax.rem(at[axis] + i, 4) for i in (1, 2, 3)]

    sibling = (band + 1 - 2 * core, sector)
    peers = [place("x", i) for i in others("x")] + [place("z", i) for i in others("z")]
    peers += [place("y", lax.rem(sector + 2, 4))]
    barrier = pltpu.get_barrier_semaphore()
    for spot in ahead + peers:
        pl.semaphore_signal(barrier, inc=1, device_id=spot, device_id_type=MESH)
    load = pltpu.make_async_copy(grads_ref.at[core], mine_ref, load_sem)
    load.start()
    pl.semaphore_wait(barrier, len(ahead + peers))

    returns = []
    core_copy = pltpu.make_async_remote_copy(
        src_ref=grads_ref.at[1 - core], dst_ref=half_ref,
        send_sem=core_sem.at[0], recv_sem=core_sem.at[1],
        device_id=sibling, device_id_type=MESH,
    )
    core_copy.start()
    for j in range(8):
        returns.append(
            pltpu.make_async_remote_copy(
                src_ref=back_ref.at[j], dst_ref=arrived_ref.at[j],
                send_sem=back_send.at[j], recv_sem=back_recv.at[j],
                device_id=ahead[j], device_id_type=MESH,
            )
        )
        returns[-1].start()

    orders = (("x", "y", "z"), ("y", "z", "x"), ("z", "x", "y"))
    starts = [16 * sum(share[:p]) for p in range(3)]

    def exchange(stage, p, axis, source, target):
        copies = []
        for i, other in enumerate(others(axis)):
            copies.append(
                pltpu.make_async_remote_copy(
                    src_ref=source(other, i), dst_ref=target(i),
                    send_sem=send_sem.at[stage, p, i], recv_sem=recv_sem.at[stage, p, i],
                    device_id=place(axis, other), device_id_type=MESH,
                )
            )
            copies[-1].start()
        return copies

    def finish(copies):
        for copy in copies:
            copy.wait()

    load.wait()
    core_copy.wait()
    one_ref[...] = (mine_ref[...].astype(F32) + half_ref[...].astype(F32)).astype(BF16)

    live = []
    for p in range(3):
        m, axis = share[p], orders[p][0]
        live.append(exchange(
            0, p, axis,
            lambda other, i, p=p, m=m: one_ref.at[pl.ds(starts[p] + other * (4 * m), 4 * m)],
            lambda i, p=p, m=m: first_in.at[i, pl.ds(4 * sum(share[:p]), 4 * m)],
        ))
    for p in range(3):
        m, axis, low = share[p], orders[p][0], 4 * sum(share[:p])
        finish(live[p])
        total = one_ref[pl.ds(starts[p] + at[axis] * (4 * m), 4 * m)].astype(F32)
        for i in range(3):
            total += first_in[i, low : low + 4 * m].astype(F32)
        two_ref[low : low + 4 * m] = total.astype(BF16)
        live[p] = exchange(
            1, p, orders[p][1],
            lambda other, i, low=low, m=m: two_ref.at[pl.ds(low + other * m, m)],
            lambda i, p=p, m=m: second_in.at[i, pl.ds(sum(share[:p]), m)],
        )
    for p in range(3):
        m, axis, low, mid = share[p], orders[p][1], sum(share[:p]), 4 * sum(share[:p])
        finish(live[p])
        total = two_ref[pl.ds(mid + at[axis] * m, m)].astype(F32)
        for i in range(3):
            total += second_in[i, low : low + m].astype(F32)
        three_ref[low : low + m] = total.astype(BF16)
        third = orders[p][2]
        third_in[at[third], low : low + m] = total.astype(BF16)
        live[p] = exchange(
            2, p, third,
            lambda other, i, low=low, m=m: three_ref.at[pl.ds(low, m)],
            lambda i, low=low, m=m, third=third: third_in.at[at[third], pl.ds(low, m)],
        )
    for p in range(3):
        m, low = share[p], sum(share[:p])
        finish(live[p])
        total = third_in[0, low : low + m].astype(F32)
        for i in range(1, 4):
            total += third_in[i, low : low + m].astype(F32)
        spot = starts[p] + at[orders[p][0]] * (4 * m) + at[orders[p][1]] * m
        out_ref[core, pl.ds(spot, m)] = total.astype(BF16)
        live[p] = exchange(
            3, p, orders[p][1],
            lambda other, i, spot=spot, m=m: out_ref.at[core, pl.ds(spot, m)],
            lambda i, spot=spot, m=m: out_ref.at[core, pl.ds(spot, m)],
        )
    for p in range(3):
        m = share[p]
        finish(live[p])
        spot = starts[p] + at[orders[p][0]] * (4 * m)
        live[p] = exchange(
            4, p, orders[p][0],
            lambda other, i, spot=spot, m=m: out_ref.at[core, pl.ds(spot, 4 * m)],
            lambda i, spot=spot, m=m: out_ref.at[core, pl.ds(spot, 4 * m)],
        )
    last = []
    for p in range(3):
        finish(live[p])
        spot, m = starts[p], 16 * share[p]
        last.append(pltpu.make_async_remote_copy(
            src_ref=out_ref.at[core, pl.ds(spot, m)], dst_ref=out_ref.at[core, pl.ds(spot, m)],
            send_sem=core_sem.at[2 + p], recv_sem=core_sem.at[5 + p],
            device_id=sibling, device_id_type=MESH,
        ))
        last[-1].start()
    finish(returns)
    finish(last)


def sum_call(bands, sectors, back, grads):
    half = grads.shape[0] // 2
    unit = half // 16
    share = (unit - 2 * (unit // 3), unit // 3, unit // 3)
    whole = pl.BlockSpec(memory_space=pltpu.VMEM)
    there = pl.BlockSpec(memory_space=pl.ANY)
    tile = grads.shape[1:]
    return pl.pallas_call(
        functools.partial(sum_kernel, bands, sectors, share),
        in_specs=[there, there],
        out_specs=[there, whole],
        out_shape=[
            jax.ShapeDtypeStruct(back.shape, BF16),
            jax.ShapeDtypeStruct((2, half) + tile, BF16),
        ],
        scratch_shapes=[
            pltpu.VMEM((half,) + tile, BF16),
            pltpu.VMEM((half,) + tile, BF16),
            pltpu.VMEM((half // 4,) + tile, BF16),
            pltpu.VMEM((unit,) + tile, BF16),
            pltpu.VMEM((3, half // 4) + tile, BF16),
            pltpu.VMEM((3, unit) + tile, BF16),
            pltpu.VMEM((4, unit) + tile, BF16),
            pltpu.VMEM((half,) + tile, BF16),
            pltpu.SemaphoreType.DMA((5, 3, 3)),
            pltpu.SemaphoreType.DMA((5, 3, 3)),
            pltpu.SemaphoreType.DMA((8,)),
            pltpu.SemaphoreType.DMA((8,)),
            pltpu.SemaphoreType.DMA((8,)),
            pltpu.SemaphoreType.DMA,
        ],
        compiler_params=pltpu.CompilerParams(
            collective_id=1, has_side_effects=True, vmem_limit_bytes=60 * 1024 * 1024
        ),
    )(back, grads.reshape((2, half) + tile))


def close_kernel(scale, rows_ref, arrived_hbm, part_hbm, sums_hbm, ngrad_ref, *refs):
    outs, (arrived_ref, part_ref, sums_ref, sem) = refs[:4], refs[4:]
    loads = [
        pltpu.make_async_copy(part_hbm, part_ref, sem.at[0]),
        pltpu.make_async_copy(arrived_hbm, arrived_ref, sem.at[1]),
        pltpu.make_async_copy(sums_hbm, sums_ref, sem.at[2]),
    ]
    for load in loads:
        load.start()
    n = part_ref.shape[0]
    chosen = [picked(rows_ref[0, j : j + 1, :], n) for j in range(8)]
    loads[0].wait()
    loads[1].wait()
    total = part_ref[...]
    for j in range(8):
        total += dot(chosen[j], arrived_ref[j])
    ngrad_ref[...] = total
    loads[2].wait()
    at = 0
    for out in outs:
        for i in range(out.shape[0] // 16):
            for j in range(out.shape[1] // 128):
                out[16 * i : 16 * i + 16, 128 * j : 128 * j + 128] = sums_ref[at].astype(F32) * scale
                at += 1


def close_call(scale, rows, arrived, part, sums):
    d = part.shape[1]
    whole = pl.BlockSpec(memory_space=pltpu.VMEM)
    there = pl.BlockSpec(memory_space=pl.ANY)
    outs = [part.shape, (3 * d, d), (d, d), (2 * d, d), (d, d)]
    sums = sums.reshape((-1,) + sums.shape[2:])
    return pl.pallas_call(
        functools.partial(close_kernel, scale),
        in_specs=[whole, there, there, there],
        out_specs=[whole] * 5,
        out_shape=[jax.ShapeDtypeStruct(shape, F32) for shape in outs],
        scratch_shapes=[
            pltpu.VMEM(arrived.shape, BF16),
            pltpu.VMEM(part.shape, F32),
            pltpu.VMEM(sums.shape, BF16),
            pltpu.SemaphoreType.DMA((3,)),
        ],
        compiler_params=pltpu.CompilerParams(vmem_limit_bytes=60 * 1024 * 1024),
    )(rows, arrived, part, sums)


def solution(mesh):
    bands, sectors = mesh.shape["band"], mesh.shape["sector"]

    def local(node, edge, slot, mask, rows, w_ein, b_e, w_eout, g_e, w_nin, b_n, w_nout, g_n, ncot, ecot):
        n, d = node.shape
        far = fetch_call(bands, sectors, node, rows)
        nnew, enew, egrad, part, back, grads = layer_call(
            node, far.reshape(-1, d), edge, slot, mask,
            w_ein, b_e, w_eout, g_e, w_nin, b_n, w_nout, g_n, ncot, ecot,
        )
        arrived, sums = sum_call(bands, sectors, back, grads)
        scale = float(bands * sectors * n * slot.shape[1]) ** (-0.5)
        outs = close_call(scale, rows, arrived, part, sums)
        return (nnew, enew, outs[0], egrad) + tuple(outs[1:])

    split = P(("band", "sector"), None)
    in_specs = (split,) * 4 + (P(("band", "sector"), None, None),) + (P(),) * 8 + (split, split)
    out_specs = (split,) * 4 + (P(),) * 4
    return jax.shard_map(local, mesh=mesh, in_specs=in_specs, out_specs=out_specs, check_vma=False)
```

```python
import functools
import jax
import jax.numpy as jnp
from jax import lax
from jax.experimental import pallas as pl
from jax.experimental.pallas import tpu as pltpu
from jax.sharding import PartitionSpec as P

F32, BF16 = jnp.float32, jnp.bfloat16
R = 64
SUB = 4
D = 256


def dot(a, b):
    return jnp.dot(a, b, preferred_element_type=F32)


def dot_rows(a, b):
    return lax.dot_general(a, b, (((0,), (0,)), ((), ())), preferred_element_type=F32)


def silu_parts(pre):
    gate = 0.5 * jnp.tanh(0.5 * pre) + 0.5
    hidden = pre * gate
    return hidden, gate + hidden * (1.0 - gate)


def centred(matrix):
    return matrix - jnp.mean(matrix, 1, keepdims=True)


def flipped(matrix):
    return jnp.transpose(matrix.astype(F32)).astype(BF16)


def layer_kernel(
    steps, slots,
    own_ref, far_ref, edge_ref, slot_ref, mask_ref,
    w_ein, b_e, w_eout, g_e, nin_hbm, b_n, nout_hbm, g_n, ncot_hbm, ecot_ref,
    nnew_hbm, enew_ref, egrad_hbm, ngrad_hbm, back_hbm, grads_ref,
    x_ref, xt_ref, g_ref, dz_ref, dpre_ref, wcat_ref, weo_ref, weot_ref, wet_ref, recv_ref, value_ref, parts_ref, partst_ref,
    sel_ref, line_ref, hid_ref, dsil_ref, xh_ref, rm_ref, gath_ref, dgath_ref,
    acc_ref, gout_ref, gd_ref, down_ref, gnode_ref,
    egrad_ref, w_nin, w_nout, ncot_ref, nnew_ref, back_ref, egrad_sem, node_sem,
):
    t = pl.program_id(0)
    rows = R * slots
    n = own_ref.shape[0]
    table = n + far_ref.shape[0]
    seg = D + table

    def spread_rows(ref, base):
        upper = lax.broadcasted_iota(jnp.int32, (8, ref.shape[1]), 0) < 4
        pieces = []
        for pair in range(R // 2):
            a = jnp.broadcast_to(ref[pl.ds(base + 2 * pair, 1), :], (8, ref.shape[1]))
            b = jnp.broadcast_to(ref[pl.ds(base + 2 * pair + 1, 1), :], (8, ref.shape[1]))
            pieces += [a, jnp.where(upper, a, b), b]
        return jnp.concatenate(pieces, axis=0)

    late = [
        pltpu.make_async_copy(nin_hbm, w_nin, node_sem.at[0]),
        pltpu.make_async_copy(nout_hbm, w_nout, node_sem.at[1]),
        pltpu.make_async_copy(ncot_hbm, ncot_ref, node_sem.at[2]),
    ]
    nnew_copy = pltpu.make_async_copy(nnew_ref, nnew_hbm, node_sem.at[3])
    down_copy = pltpu.make_async_copy(down_ref, ngrad_hbm, node_sem.at[4])
    back_copy = pltpu.make_async_copy(back_ref, back_hbm, node_sem.at[5])

    def egrad_copy(step, s):
        span = pl.ds(pl.multiple_of((step * SUB + s) * rows, rows), rows)
        return pltpu.make_async_copy(egrad_ref.at[s * rows : (s + 1) * rows, :], egrad_hbm.at[span, :], egrad_sem.at[s])

    @pl.when(t == 0)
    def _():
        for copy in late:
            copy.start()
        e = lax.broadcasted_iota(jnp.int32, (R, rows), 1)
        r = lax.broadcasted_iota(jnp.int32, (R, rows), 0)
        gap = e - slots * r
        inside = (gap >= 0) & (gap < slots)
        g_ref[...] = jnp.where(inside, 1.0, 0.0).astype(BF16)
        ef = lax.broadcasted_iota(jnp.int32, (32, rows), 1).astype(F32)
        lf = lax.broadcasted_iota(jnp.int32, (32, rows), 0).astype(F32)
        k = ef - slots * jnp.floor((ef + 0.5) * (1.0 / slots))
        selt = jnp.where(lf == k, 32.0, 0.0) + jnp.where(lf == k + 16.0, 1.0, 0.0)
        ef = lax.broadcasted_iota(jnp.int32, (rows, 128), 0).astype(F32)
        lf = lax.broadcasted_iota(jnp.int32, (rows, 128), 1).astype(F32)
        k = ef - slots * jnp.floor((ef + 0.5) * (1.0 / slots))
        sel_ref[...] = jnp.where(lf == k, 1.0, 0.0)
        v = slot_ref[...] + 1024 * mask_ref[...]
        partst_ref[...] = jnp.zeros_like(partst_ref)
        partst_ref[0:slots, :] = v.astype(F32)
        value_ref[...] = jnp.transpose(partst_ref[...])
        high = (v >> 5).astype(F32)
        low = (v & 31).astype(F32)
        parts_ref[...] = jnp.zeros_like(parts_ref)
        parts_ref[0:16, :] = jnp.concatenate([high, jnp.zeros((16 - slots, n), F32)], axis=0).astype(BF16)
        parts_ref[16:32, :] = jnp.concatenate([low, jnp.zeros((16 - slots, n), F32)], axis=0).astype(BF16)
        for tile in range(n // R):
            piece = dot(parts_ref[0:32, tile * R : tile * R + R], g_ref[...])
            line_ref[tile] = jnp.sum(piece * selt, 0, keepdims=True)
        wcat_ref[0:D, :] = w_ein[0:D, :]
        wcat_ref[D : D + n, :] = dot(own_ref[...], w_ein[D : 2 * D, :]).astype(BF16)
        wcat_ref[D + n : seg, :] = dot(far_ref[...], w_ein[D : 2 * D, :]).astype(BF16)
        recv_ref[...] = dot(own_ref[...], w_ein[2 * D :, :]) + b_e[...]
        weo = centred(w_eout[...].astype(F32))
        weo_ref[...] = weo.astype(BF16)
        weot_ref[...] = jnp.transpose(weo).astype(BF16)
        wet_ref[...] = flipped(w_ein[0:D, :])
        acc_ref[...] = jnp.zeros_like(acc_ref)
        gout_ref[...] = jnp.zeros_like(gout_ref)

    def spots(step, s):
        at = step * (R * SUB) + s * R
        here = pl.ds(pl.multiple_of(at * slots, rows), rows)
        mine = pl.ds(pl.multiple_of(at, R), R)
        return here, mine, slice(s * rows, (s + 1) * rows)

    def first_half(s):
        here, mine, part = spots(t, s)
        x = x_ref.at[s]
        x[:, 0:D] = edge_ref[part, :]
        base = pl.multiple_of(t * (R * SUB) + s * R, R)
        v = jnp.sum(spread_rows(value_ref, base) * sel_ref[...], 1, keepdims=True)
        real = v >= 1024.0
        slot = jnp.where(real, v - 1024.0, v)
        lane = lax.broadcasted_iota(jnp.int32, (rows, D), 1).astype(F32).astype(BF16)
        for block in range(table // D):
            wanted = (slot - float(block * D)).astype(BF16)
            x[:, D + block * D : 2 * D + block * D] = jnp.where(
                lane == wanted, jnp.ones((), BF16), jnp.zeros((), BF16)
            )
        pre = dot(x[...], wcat_ref[...]) + spread_rows(recv_ref, base)
        return pre, jnp.where(real, 1.0, 0.0)

    def second_half(s, pre, keep):
        here, mine, part = spots(t, s)
        hidden, slope = silu_parts(pre)
        hidden = hidden.astype(BF16)
        hid_ref[here, :] = hidden
        dsil_ref[here, :] = slope.astype(BF16)
        c = dot(hidden, weo_ref[...])
        rstd = lax.rsqrt(jnp.mean(c * c, 1, keepdims=True) + 1e-05)
        normed = c * rstd
        xh_ref[here, :] = normed.astype(BF16)
        rm_ref[here, :] = rstd * keep
        update = normed * g_e[...] * keep
        enew_ref[part, :] = (edge_ref[part, :].astype(F32) + update).astype(BF16)
        gath_ref[mine, :] = dot(g_ref[...], update.astype(BF16)).astype(BF16)

    @pl.when(t < steps)
    def _():
        held = first_half(0)
        for s in range(1, SUB):
            following = first_half(s)
            second_half(s - 1, *held)
            held = following
        second_half(SUB - 1, *held)

    @pl.when(t == steps)
    def _():
        for copy in late:
            copy.wait()
        own = own_ref[...]
        gath = gath_ref[...]
        pre = dot(own, w_nin[0:D, :]) + dot(gath, w_nin[D:, :]) + b_n[...]
        hidden, slope = silu_parts(pre)
        hidden = hidden.astype(BF16)
        wno = centred(w_nout[...].astype(F32))
        c = dot(hidden, wno.astype(BF16))
        rstd = lax.rsqrt(jnp.mean(c * c, 1, keepdims=True) + 1e-05)
        normed = c * rstd
        nnew_ref[...] = (own.astype(F32) + normed * g_n[...]).astype(BF16)
        nnew_copy.start()
        cot = ncot_ref[...].astype(F32)
        dx = cot * g_n[...]
        share = jnp.mean(dx * normed, 1, keepdims=True)
        dz = (rstd * (dx - normed * share)).astype(BF16)
        gnode_ref[2 * D : 3 * D, :] = centred(dot_rows(hidden, dz))
        dpre = (dot(dz, jnp.transpose(wno).astype(BF16)) * slope).astype(BF16)
        gnode_ref[0:D, :] = dot_rows(own, dpre)
        gnode_ref[D : 2 * D, :] = dot_rows(gath, dpre)
        down_ref[...] = cot + dot(dpre, flipped(w_nin[0:D, :]))
        dgath_ref[...] = dot(dpre, flipped(w_nin[D:, :]))

    def third_half(s):
        here, mine, part = spots(t - steps - 1, s)
        v = line_ref[(t - steps - 1) * SUB + s]
        slot = jnp.where(v >= 1024.0, v - 1024.0, v)
        xt_ref[0:D, part] = jnp.transpose(edge_ref[part, :])
        line = lax.broadcasted_iota(jnp.int32, (D, rows), 0).astype(F32).astype(BF16)
        for block in range(table // D):
            wanted = (slot - float(block * D)).astype(BF16)
            xt_ref[D + block * D : 2 * D + block * D, part] = jnp.where(
                line == wanted, jnp.ones((), BF16), jnp.zeros((), BF16)
            )
        cot = ecot_ref[part, :].astype(F32)
        base = pl.multiple_of((t - steps - 1) * (R * SUB) + s * R, R)
        dx = (cot + spread_rows(dgath_ref, base)) * g_e[...]
        normed = xh_ref[here, :].astype(F32)
        share_of = jnp.mean(dx * normed, 1, keepdims=True)
        dz = (rm_ref[here, :] * (dx - normed * share_of)).astype(BF16)
        dz_ref[part, :] = dz
        dpre = (dot(dz, weot_ref[...]) * dsil_ref[here, :].astype(F32)).astype(BF16)
        dpre_ref[part, :] = dpre
        egrad_ref[part, :] = (cot + dot(dpre, wet_ref[...])).astype(BF16)
        egrad_copy(t - steps - 1, s).start()
        gd_ref[mine, :] = dot(g_ref[...], dpre).astype(BF16)

    @pl.when(t > steps + 1)
    def _():
        for s in range(SUB):
            egrad_copy(t - steps - 2, s).wait()

    @pl.when(t > steps)
    def _():
        for s in range(SUB):
            third_half(s)
        span = pl.ds(pl.multiple_of((t - steps - 1) * (rows * SUB), rows), rows * SUB)
        gout_ref[...] += dot_rows(hid_ref[span, :], dz_ref[...])
        acc_ref[...] += dot(xt_ref[...], dpre_ref[...])

    @pl.when(t == 2 * steps)
    def _():
        own = own_ref[...]
        near = acc_ref[D : D + n, :].astype(BF16)
        far = acc_ref[D + n : seg, :].astype(BF16)
        wst = flipped(w_ein[D : 2 * D, :])
        back_ref[...] = dot(far, wst).astype(BF16).reshape(back_ref.shape)
        back_copy.start()
        gd = gd_ref[...]
        down_ref[...] += dot(near, wst) + dot(gd, flipped(w_ein[2 * D :, :]))
        down_copy.start()
        g_s = dot_rows(own, near) + dot_rows(far_ref[...], far)
        g_r = dot_rows(own, gd)
        whole = [acc_ref[0:D, :], g_s, g_r, centred(gout_ref[...])]
        whole += [gnode_ref[i * D : (i + 1) * D, :] for i in range(3)]
        at = 0
        for piece in whole:
            for i in range(D // 16):
                for j in range(2):
                    grads_ref[at] = piece[16 * i : 16 * i + 16, 128 * j : 128 * j + 128].astype(BF16)
                    at += 1
        for s in range(SUB):
            egrad_copy(steps - 1, s).wait()
        for copy in (nnew_copy, down_copy, back_copy):
            copy.wait()


def layer_call(node, far, edge, slot, mask, w_ein, b_e, w_eout, g_e, w_nin, b_n, w_nout, g_n, ncot, ecot):
    n, d = node.shape
    slots = slot.shape[1]
    rows = R * slots
    tiles = n // (R * SUB)
    table = n + far.shape[0]
    seg = d + table
    total = n * slots
    whole = pl.BlockSpec(memory_space=pltpu.VMEM)
    there = pl.BlockSpec(memory_space=pl.ANY)
    stream_e = pl.BlockSpec((rows * SUB, d), lambda t: (jnp.where(t < tiles, t, jnp.maximum(t - tiles - 1, 0)), 0))
    first = pl.BlockSpec((rows * SUB, d), lambda t: (jnp.minimum(t, tiles - 1), 0))
    second = pl.BlockSpec((rows * SUB, d), lambda t: (jnp.maximum(t - tiles - 1, 0), 0))
    tiles_all = 7 * (d // 16) * (d // 128)
    flops = 2 * total * d * (d * 8 + 2 * table)
    return pl.pallas_call(
        functools.partial(layer_kernel, tiles, slots),
        grid=(2 * tiles + 1,),
        in_specs=[whole, whole, stream_e] + [whole] * 6 + [there, whole, there, whole, there, second],
        out_specs=[there, first, there, there, there, whole],
        out_shape=[
            jax.ShapeDtypeStruct((n, d), BF16),
            jax.ShapeDtypeStruct((total, d), BF16),
            jax.ShapeDtypeStruct((total, d), BF16),
            jax.ShapeDtypeStruct((n, d), F32),
            jax.ShapeDtypeStruct((8, far.shape[0] // 8, d), BF16),
            jax.ShapeDtypeStruct((tiles_all, 16, 128), BF16),
        ],
        scratch_shapes=[
            pltpu.VMEM((SUB, rows, seg), BF16),
            pltpu.VMEM((seg, SUB * rows), BF16),
            pltpu.VMEM((R, rows), BF16),
            pltpu.VMEM((SUB * rows, d), BF16),
            pltpu.VMEM((SUB * rows, d), BF16),
            pltpu.VMEM((seg, d), BF16),
            pltpu.VMEM((d, d), BF16),
            pltpu.VMEM((d, d), BF16),
            pltpu.VMEM((d, d), BF16),
            pltpu.VMEM((n, d), F32),
            pltpu.VMEM((n, 128), F32),
            pltpu.VMEM((32, n), BF16),
            pltpu.VMEM((128, n), F32),
            pltpu.VMEM((rows, 128), F32),
            pltpu.VMEM((n // R, 1, rows), F32),
            pltpu.VMEM((total, d), BF16),
            pltpu.VMEM((total, d), BF16),
            pltpu.VMEM((total, d), BF16),
            pltpu.VMEM((total, 1), F32),
            pltpu.VMEM((n, d), BF16),
            pltpu.VMEM((n, d), F32),
            pltpu.VMEM((seg, d), F32),
            pltpu.VMEM((d, d), F32),
            pltpu.VMEM((n, d), BF16),
            pltpu.VMEM((n, d), F32),
            pltpu.VMEM((3 * d, d), F32),
            pltpu.VMEM((SUB * rows, d), BF16),
            pltpu.VMEM((2 * d, d), BF16),
            pltpu.VMEM((d, d), BF16),
            pltpu.VMEM((n, d), BF16),
            pltpu.VMEM((n, d), BF16),
            pltpu.VMEM((8, far.shape[0] // 8, d), BF16),
            pltpu.SemaphoreType.DMA((SUB,)),
            pltpu.SemaphoreType.DMA((6,)),
        ],
        compiler_params=pltpu.CompilerParams(vmem_limit_bytes=60 * 1024 * 1024),
        cost_estimate=pl.CostEstimate(flops=flops, bytes_accessed=5 * total * d * 2, transcendentals=total * d),
    )(node, far, edge, slot.T, mask.T, w_ein, b_e.reshape(1, -1), w_eout, g_e.reshape(1, -1), w_nin, b_n.reshape(1, -1), w_nout, g_n.reshape(1, -1), ncot, ecot)


band_steps = (-1, -1, -1, 0, 0, 1, 1, 1)
sector_steps = (-1, 0, 1, -1, 1, -1, 0, 1)
MESH = pl.DeviceIdType.MESH


def neighbours(bands, sectors):
    band, sector = lax.axis_index("band"), lax.axis_index("sector")
    ahead = [
        (lax.rem(band + b + bands, bands), lax.rem(sector + s + sectors, sectors))
        for b, s in zip(band_steps, sector_steps)
    ]
    return ahead


def picked(wanted, count):
    line = lax.broadcasted_iota(jnp.int32, (count, wanted.shape[1]), 0)
    return jnp.where(line == wanted, 1.0, 0.0).astype(BF16)


def fetch_kernel(
    bands, sectors, node_hbm, rows_ref, far_ref, out_ref, node_ref, send_sem, recv_sem, load_sem
):
    ahead = neighbours(bands, sectors)
    barrier = pltpu.get_barrier_semaphore()
    for place in ahead:
        pl.semaphore_signal(barrier, inc=1, device_id=place, device_id_type=MESH)
    load = pltpu.make_async_copy(node_hbm, node_ref, load_sem)
    load.start()
    load.wait()
    node = node_ref[...]
    for j in range(8):
        choice = picked(rows_ref[0, j : j + 1, :], node.shape[0])
        out_ref[j] = dot_rows(choice, node).astype(BF16)
    pl.semaphore_wait(barrier, 8)
    copies = []
    for j in range(8):
        copies.append(
            pltpu.make_async_remote_copy(
                src_ref=out_ref.at[j],
                dst_ref=far_ref.at[j],
                send_sem=send_sem.at[j],
                recv_sem=recv_sem.at[j],
                device_id=ahead[7 - j],
                device_id_type=MESH,
            )
        )
        copies[-1].start()
    for copy in copies:
        copy.wait()


def fetch_call(bands, sectors, node, rows):
    cap, d = rows.shape[2], node.shape[1]
    whole = pl.BlockSpec(memory_space=pltpu.VMEM)
    there = pl.BlockSpec(memory_space=pl.ANY)
    return pl.pallas_call(
        functools.partial(fetch_kernel, bands, sectors),
        in_specs=[there, whole],
        out_specs=there,
        out_shape=jax.ShapeDtypeStruct((8, cap, d), BF16),
        scratch_shapes=[
            pltpu.VMEM((8, cap, d), BF16),
            pltpu.VMEM(node.shape, BF16),
            pltpu.SemaphoreType.DMA((8,)),
            pltpu.SemaphoreType.DMA((8,)),
            pltpu.SemaphoreType.DMA,
        ],
        compiler_params=pltpu.CompilerParams(
            collective_id=0, has_side_effects=True, vmem_limit_bytes=60 * 1024 * 1024
        ),
    )(node, rows)


def sum_kernel(
    bands, sectors, share, back_ref, grads_ref, arrived_ref, out_ref,
    half_ref, one_ref, two_ref, three_ref, first_in, second_in, third_in,
    mine_ref, send_sem, recv_sem, core_sem, back_send, back_recv, load_sem,
):
    ahead = neighbours(bands, sectors)
    band, sector = lax.axis_index("band"), lax.axis_index("sector")
    core = lax.rem(band, 2)
    x = lax.rem(band // 2, 4)
    z = band // 8
    at = {"x": x, "y": sector, "z": z}

    def place(axis, index):
        if axis == "x":
            return ((z * 4 + index) * 2 + core, sector)
        if axis == "z":
            return ((index * 4 + x) * 2 + core, sector)
        return (band, index)

    def others(axis):
        return [lax.rem(at[axis] + i, 4) for i in (1, 2, 3)]

    sibling = (band + 1 - 2 * core, sector)
    peers = [place("x", i) for i in others("x")] + [place("z", i) for i in others("z")]
    peers += [place("y", lax.rem(sector + 2, 4))]
    barrier = pltpu.get_barrier_semaphore()
    for spot in ahead + peers:
        pl.semaphore_signal(barrier, inc=1, device_id=spot, device_id_type=MESH)
    load = pltpu.make_async_copy(grads_ref.at[core], mine_ref, load_sem)
    load.start()
    pl.semaphore_wait(barrier, len(ahead + peers))

    returns = []
    core_copy = pltpu.make_async_remote_copy(
        src_ref=grads_ref.at[1 - core], dst_ref=half_ref,
        send_sem=core_sem.at[0], recv_sem=core_sem.at[1],
        device_id=sibling, device_id_type=MESH,
    )
    core_copy.start()
    for j in range(8):
        returns.append(
            pltpu.make_async_remote_copy(
                src_ref=back_ref.at[j], dst_ref=arrived_ref.at[j],
                send_sem=back_send.at[j], recv_sem=back_recv.at[j],
                device_id=ahead[j], device_id_type=MESH,
            )
        )
        returns[-1].start()

    orders = (("x", "y", "z"), ("y", "z", "x"), ("z", "x", "y"))
    starts = [16 * sum(share[:p]) for p in range(3)]

    def exchange(stage, p, axis, source, target):
        copies = []
        for i, other in enumerate(others(axis)):
            copies.append(
                pltpu.make_async_remote_copy(
                    src_ref=source(other, i), dst_ref=target(i),
                    send_sem=send_sem.at[stage, p, i], recv_sem=recv_sem.at[stage, p, i],
                    device_id=place(axis, other), device_id_type=MESH,
                )
            )
            copies[-1].start()
        return copies

    def finish(copies):
        for copy in copies:
            copy.wait()

    load.wait()
    core_copy.wait()
    one_ref[...] = (mine_ref[...].astype(F32) + half_ref[...].astype(F32)).astype(BF16)

    live = []
    for p in range(3):
        m, axis = share[p], orders[p][0]
        live.append(exchange(
            0, p, axis,
            lambda other, i, p=p, m=m: one_ref.at[pl.ds(starts[p] + other * (4 * m), 4 * m)],
            lambda i, p=p, m=m: first_in.at[i, pl.ds(4 * sum(share[:p]), 4 * m)],
        ))
    for p in range(3):
        m, axis, low = share[p], orders[p][0], 4 * sum(share[:p])
        finish(live[p])
        total = one_ref[pl.ds(starts[p] + at[axis] * (4 * m), 4 * m)].astype(F32)
        for i in range(3):
            total += first_in[i, low : low + 4 * m].astype(F32)
        two_ref[low : low + 4 * m] = total.astype(BF16)
        live[p] = exchange(
            1, p, orders[p][1],
            lambda other, i, low=low, m=m: two_ref.at[pl.ds(low + other * m, m)],
            lambda i, p=p, m=m: second_in.at[i, pl.ds(sum(share[:p]), m)],
        )
    for p in range(3):
        m, axis, low, mid = share[p], orders[p][1], sum(share[:p]), 4 * sum(share[:p])
        finish(live[p])
        total = two_ref[pl.ds(mid + at[axis] * m, m)].astype(F32)
        for i in range(3):
            total += second_in[i, low : low + m].astype(F32)
        three_ref[low : low + m] = total.astype(BF16)
        third = orders[p][2]
        third_in[at[third], low : low + m] = total.astype(BF16)
        live[p] = exchange(
            2, p, third,
            lambda other, i, low=low, m=m: three_ref.at[pl.ds(low, m)],
            lambda i, low=low, m=m, third=third: third_in.at[at[third], pl.ds(low, m)],
        )
    for p in range(3):
        m, low = share[p], sum(share[:p])
        finish(live[p])
        total = third_in[0, low : low + m].astype(F32)
        for i in range(1, 4):
            total += third_in[i, low : low + m].astype(F32)
        spot = starts[p] + at[orders[p][0]] * (4 * m) + at[orders[p][1]] * m
        out_ref[core, pl.ds(spot, m)] = total.astype(BF16)
        live[p] = exchange(
            3, p, orders[p][1],
            lambda other, i, spot=spot, m=m: out_ref.at[core, pl.ds(spot, m)],
            lambda i, spot=spot, m=m: out_ref.at[core, pl.ds(spot, m)],
        )
    for p in range(3):
        m = share[p]
        finish(live[p])
        spot = starts[p] + at[orders[p][0]] * (4 * m)
        live[p] = exchange(
            4, p, orders[p][0],
            lambda other, i, spot=spot, m=m: out_ref.at[core, pl.ds(spot, 4 * m)],
            lambda i, spot=spot, m=m: out_ref.at[core, pl.ds(spot, 4 * m)],
        )
    last = []
    for p in range(3):
        finish(live[p])
        spot, m = starts[p], 16 * share[p]
        last.append(pltpu.make_async_remote_copy(
            src_ref=out_ref.at[core, pl.ds(spot, m)], dst_ref=out_ref.at[core, pl.ds(spot, m)],
            send_sem=core_sem.at[2 + p], recv_sem=core_sem.at[5 + p],
            device_id=sibling, device_id_type=MESH,
        ))
        last[-1].start()
    finish(returns)
    finish(last)


def sum_call(bands, sectors, back, grads):
    half = grads.shape[0] // 2
    unit = half // 16
    share = (unit - 2 * (unit // 3), unit // 3, unit // 3)
    whole = pl.BlockSpec(memory_space=pltpu.VMEM)
    there = pl.BlockSpec(memory_space=pl.ANY)
    tile = grads.shape[1:]
    return pl.pallas_call(
        functools.partial(sum_kernel, bands, sectors, share),
        in_specs=[there, there],
        out_specs=[there, whole],
        out_shape=[
            jax.ShapeDtypeStruct(back.shape, BF16),
            jax.ShapeDtypeStruct((2, half) + tile, BF16),
        ],
        scratch_shapes=[
            pltpu.VMEM((half,) + tile, BF16),
            pltpu.VMEM((half,) + tile, BF16),
            pltpu.VMEM((half // 4,) + tile, BF16),
            pltpu.VMEM((unit,) + tile, BF16),
            pltpu.VMEM((3, half // 4) + tile, BF16),
            pltpu.VMEM((3, unit) + tile, BF16),
            pltpu.VMEM((4, unit) + tile, BF16),
            pltpu.VMEM((half,) + tile, BF16),
            pltpu.SemaphoreType.DMA((5, 3, 3)),
            pltpu.SemaphoreType.DMA((5, 3, 3)),
            pltpu.SemaphoreType.DMA((8,)),
            pltpu.SemaphoreType.DMA((8,)),
            pltpu.SemaphoreType.DMA((8,)),
            pltpu.SemaphoreType.DMA,
        ],
        compiler_params=pltpu.CompilerParams(
            collective_id=1, has_side_effects=True, vmem_limit_bytes=60 * 1024 * 1024
        ),
    )(back, grads.reshape((2, half) + tile))


def close_kernel(scale, rows_ref, arrived_hbm, part_hbm, sums_hbm, *refs):
    targets, (arrived_ref, part_ref, sums_ref, ngrad_ref), outs = refs[:5], refs[5:9], refs[9:13]
    load_sem, store_sem = refs[13:]
    spans, at = [], 0
    for out in outs:
        size = out.shape[0] // 8
        spans.append((at, size))
        at += size
    loads = [
        pltpu.make_async_copy(sums_hbm.at[start : start + size], sums_ref.at[start : start + size], load_sem.at[i])
        for i, (start, size) in enumerate(spans)
    ]
    loads.append(pltpu.make_async_copy(part_hbm, part_ref, load_sem.at[4]))
    loads.append(pltpu.make_async_copy(arrived_hbm, arrived_ref, load_sem.at[5]))
    for load in loads:
        load.start()
    stores = [
        pltpu.make_async_copy(ref, target, store_sem.at[i])
        for i, (ref, target) in enumerate(zip(outs + (ngrad_ref,), targets[1:] + targets[:1]))
    ]
    n = part_ref.shape[0]
    chosen = [picked(rows_ref[0, j : j + 1, :], n) for j in range(8)]
    for i, (out, (start, size)) in enumerate(zip(outs, spans)):
        loads[i].wait()
        for tile in range(size):
            r, l = 16 * (tile // 2), 128 * (tile % 2)
            out[r : r + 16, l : l + 128] = sums_ref[start + tile].astype(F32) * scale
        stores[i].start()
    loads[4].wait()
    loads[5].wait()
    total = part_ref[...]
    for j in range(8):
        total += dot(chosen[j], arrived_ref[j])
    ngrad_ref[...] = total
    stores[4].start()
    for store in stores:
        store.wait()


def close_call(scale, rows, arrived, part, sums):
    d = part.shape[1]
    whole = pl.BlockSpec(memory_space=pltpu.VMEM)
    there = pl.BlockSpec(memory_space=pl.ANY)
    outs = [part.shape, (3 * d, d), (d, d), (2 * d, d), (d, d)]
    sums = sums.reshape((-1,) + sums.shape[2:])
    return pl.pallas_call(
        functools.partial(close_kernel, scale),
        in_specs=[whole, there, there, there],
        out_specs=[there] * 5,
        out_shape=[jax.ShapeDtypeStruct(shape, F32) for shape in outs],
        scratch_shapes=[
            pltpu.VMEM(arrived.shape, BF16),
            pltpu.VMEM(part.shape, F32),
            pltpu.VMEM(sums.shape, BF16),
        ]
        + [pltpu.VMEM(shape, F32) for shape in outs]
        + [pltpu.SemaphoreType.DMA((6,)), pltpu.SemaphoreType.DMA((5,))],
        compiler_params=pltpu.CompilerParams(vmem_limit_bytes=60 * 1024 * 1024),
    )(rows, arrived, part, sums)


def solution(mesh):
    bands, sectors = mesh.shape["band"], mesh.shape["sector"]

    def local(node, edge, slot, mask, rows, w_ein, b_e, w_eout, g_e, w_nin, b_n, w_nout, g_n, ncot, ecot):
        n, d = node.shape
        far = fetch_call(bands, sectors, node, rows)
        nnew, enew, egrad, part, back, grads = layer_call(
            node, far.reshape(-1, d), edge, slot, mask,
            w_ein, b_e, w_eout, g_e, w_nin, b_n, w_nout, g_n, ncot, ecot,
        )
        arrived, sums = sum_call(bands, sectors, back, grads)
        scale = float(bands * sectors * n * slot.shape[1]) ** (-0.5)
        outs = close_call(scale, rows, arrived, part, sums)
        return (nnew, enew, outs[0], egrad) + tuple(outs[1:])

    split = P(("band", "sector"), None)
    in_specs = (split,) * 4 + (P(("band", "sector"), None, None),) + (P(),) * 8 + (split, split)
    out_specs = (split,) * 4 + (P(),) * 4
    return jax.shard_map(local, mesh=mesh, in_specs=in_specs, out_specs=out_specs, check_vma=False)
```

```python
import functools
import jax
import jax.numpy as jnp
from jax import lax
from jax.experimental import pallas as pl
from jax.experimental.pallas import tpu as pltpu
from jax.sharding import PartitionSpec as P

F32, BF16 = jnp.float32, jnp.bfloat16
R = 64
SUB = 4
D = 256


def dot(a, b):
    return jnp.dot(a, b, preferred_element_type=F32)


def dot_rows(a, b):
    return lax.dot_general(a, b, (((0,), (0,)), ((), ())), preferred_element_type=F32)


def silu_parts(pre):
    gate = 0.5 * jnp.tanh(0.5 * pre) + 0.5
    hidden = pre * gate
    return hidden, gate + hidden * (1.0 - gate)


def centred(matrix):
    return matrix - jnp.mean(matrix, 1, keepdims=True)


def flipped(matrix):
    return jnp.transpose(matrix.astype(F32)).astype(BF16)


def spread_rows(ref, base):
    upper = lax.broadcasted_iota(jnp.int32, (8, ref.shape[1]), 0) < 4
    pieces = []
    for pair in range(R // 2):
        a = jnp.broadcast_to(ref[pl.ds(base + 2 * pair, 1), :], (8, ref.shape[1]))
        b = jnp.broadcast_to(ref[pl.ds(base + 2 * pair + 1, 1), :], (8, ref.shape[1]))
        pieces += [a, jnp.where(upper, a, b), b]
    return jnp.concatenate(pieces, axis=0)


def slot_lanes(rows, slots):
    ef = lax.broadcasted_iota(jnp.int32, (rows, 128), 0).astype(F32)
    lf = lax.broadcasted_iota(jnp.int32, (rows, 128), 1).astype(F32)
    k = ef - slots * jnp.floor((ef + 0.5) * (1.0 / slots))
    return jnp.where(lf == k, 1.0, 0.0)


def layer_kernel(
    steps, slots,
    own_ref, far_ref, near_ref, edge_ref, slot_ref, mask_ref,
    w_ein, w_eout, g_e, nin_hbm, b_n, nout_hbm, g_n, ncot_hbm, ecot_ref,
    nnew_hbm, enew_ref, egrad_hbm, ngrad_hbm, back_hbm, grads_ref,
    x_ref, xt_ref, g_ref, dz_ref, dpre_ref, wcat_ref, weo_ref, weot_ref, wet_ref, value_ref, parts_ref, partst_ref,
    sel_ref, line_ref, hid_ref, dsil_ref, xh_ref, rm_ref, gath_ref, dgath_ref,
    acc_ref, gout_ref, gd_ref, down_ref, gnode_ref,
    egrad_ref, w_nin, w_nout, ncot_ref, nnew_ref, back_ref, egrad_sem, node_sem,
):
    t = pl.program_id(0)
    rows = R * slots
    n = own_ref.shape[0]
    table = n + far_ref.shape[0]
    seg = D + table

    late = [
        pltpu.make_async_copy(nin_hbm, w_nin, node_sem.at[0]),
        pltpu.make_async_copy(nout_hbm, w_nout, node_sem.at[1]),
        pltpu.make_async_copy(ncot_hbm, ncot_ref, node_sem.at[2]),
    ]
    nnew_copy = pltpu.make_async_copy(nnew_ref, nnew_hbm, node_sem.at[3])
    down_copy = pltpu.make_async_copy(down_ref, ngrad_hbm, node_sem.at[4])
    back_copy = pltpu.make_async_copy(back_ref, back_hbm, node_sem.at[5])

    def egrad_copy(step, s):
        span = pl.ds(pl.multiple_of((step * SUB + s) * rows, rows), rows)
        return pltpu.make_async_copy(egrad_ref.at[s * rows : (s + 1) * rows, :], egrad_hbm.at[span, :], egrad_sem.at[s])

    @pl.when(t == 0)
    def _():
        for copy in late:
            copy.start()
        e = lax.broadcasted_iota(jnp.int32, (R, rows), 1)
        r = lax.broadcasted_iota(jnp.int32, (R, rows), 0)
        gap = e - slots * r
        inside = (gap >= 0) & (gap < slots)
        g_ref[...] = jnp.where(inside, 1.0, 0.0).astype(BF16)
        ef = lax.broadcasted_iota(jnp.int32, (32, rows), 1).astype(F32)
        lf = lax.broadcasted_iota(jnp.int32, (32, rows), 0).astype(F32)
        k = ef - slots * jnp.floor((ef + 0.5) * (1.0 / slots))
        selt = jnp.where(lf == k, 32.0, 0.0) + jnp.where(lf == k + 16.0, 1.0, 0.0)
        sel_ref[...] = slot_lanes(rows, slots)
        v = slot_ref[...] + 1024 * mask_ref[...]
        partst_ref[...] = jnp.zeros_like(partst_ref)
        partst_ref[0:slots, :] = v.astype(F32)
        value_ref[...] = jnp.transpose(partst_ref[...])
        high = (v >> 5).astype(F32)
        low = (v & 31).astype(F32)
        parts_ref[...] = jnp.zeros_like(parts_ref)
        parts_ref[0:16, :] = jnp.concatenate([high, jnp.zeros((16 - slots, n), F32)], axis=0).astype(BF16)
        parts_ref[16:32, :] = jnp.concatenate([low, jnp.zeros((16 - slots, n), F32)], axis=0).astype(BF16)
        for tile in range(n // R):
            piece = dot(parts_ref[0:32, tile * R : tile * R + R], g_ref[...])
            line_ref[tile] = jnp.sum(piece * selt, 0, keepdims=True)
        wcat_ref[...] = dot(far_ref[...], w_ein[D : 2 * D, :]).astype(BF16)
        weo = centred(w_eout[...].astype(F32))
        weo_ref[...] = weo.astype(BF16)
        weot_ref[...] = jnp.transpose(weo).astype(BF16)
        wet_ref[...] = flipped(w_ein[0:D, :])
        acc_ref[...] = jnp.zeros_like(acc_ref)
        gout_ref[...] = jnp.zeros_like(gout_ref)

    def spots(step, s):
        at = step * (R * SUB) + s * R
        here = pl.ds(pl.multiple_of(at * slots, rows), rows)
        mine = pl.ds(pl.multiple_of(at, R), R)
        return here, mine, slice(s * rows, (s + 1) * rows)

    def first_half(s):
        here, mine, part = spots(t, s)
        x = x_ref.at[s]
        base = pl.multiple_of(t * (R * SUB) + s * R, R)
        v = jnp.sum(spread_rows(value_ref, base) * sel_ref[...], 1, keepdims=True)
        real = v >= 1024.0
        slot = jnp.where(real, v - 1024.0, v)
        lane = lax.broadcasted_iota(jnp.int32, (rows, D), 1).astype(F32).astype(BF16)
        for block in range((table - n) // D):
            wanted = (slot - float(n + block * D)).astype(BF16)
            x[:, block * D : D + block * D] = jnp.where(
                lane == wanted, jnp.ones((), BF16), jnp.zeros((), BF16)
            )
        pre = dot(x[...], wcat_ref[...]) + near_ref[part, :].astype(F32)
        return pre, jnp.where(real, 1.0, 0.0)

    def second_half(s, pre, keep):
        here, mine, part = spots(t, s)
        hidden, slope = silu_parts(pre)
        hidden = hidden.astype(BF16)
        hid_ref[here, :] = hidden
        dsil_ref[here, :] = slope.astype(BF16)
        c = dot(hidden, weo_ref[...])
        rstd = lax.rsqrt(jnp.mean(c * c, 1, keepdims=True) + 1e-05)
        normed = c * rstd
        xh_ref[here, :] = normed.astype(BF16)
        rm_ref[here, :] = rstd * keep
        update = normed * g_e[...] * keep
        enew_ref[part, :] = (edge_ref[part, :].astype(F32) + update).astype(BF16)
        gath_ref[mine, :] = dot(g_ref[...], update.astype(BF16)).astype(BF16)

    @pl.when(t < steps)
    def _():
        held = first_half(0)
        for s in range(1, SUB):
            following = first_half(s)
            second_half(s - 1, *held)
            held = following
        second_half(SUB - 1, *held)

    @pl.when(t == steps)
    def _():
        for copy in late:
            copy.wait()
        own = own_ref[...]
        gath = gath_ref[...]
        pre = dot(own, w_nin[0:D, :]) + dot(gath, w_nin[D:, :]) + b_n[...]
        hidden, slope = silu_parts(pre)
        hidden = hidden.astype(BF16)
        wno = centred(w_nout[...].astype(F32))
        c = dot(hidden, wno.astype(BF16))
        rstd = lax.rsqrt(jnp.mean(c * c, 1, keepdims=True) + 1e-05)
        normed = c * rstd
        nnew_ref[...] = (own.astype(F32) + normed * g_n[...]).astype(BF16)
        nnew_copy.start()
        cot = ncot_ref[...].astype(F32)
        dx = cot * g_n[...]
        share = jnp.mean(dx * normed, 1, keepdims=True)
        dz = (rstd * (dx - normed * share)).astype(BF16)
        gnode_ref[2 * D : 3 * D, :] = centred(dot_rows(hidden, dz))
        dpre = (dot(dz, jnp.transpose(wno).astype(BF16)) * slope).astype(BF16)
        gnode_ref[0:D, :] = dot_rows(own, dpre)
        gnode_ref[D : 2 * D, :] = dot_rows(gath, dpre)
        down_ref[...] = cot + dot(dpre, flipped(w_nin[0:D, :]))
        dgath_ref[...] = dot(dpre, flipped(w_nin[D:, :]))

    def third_half(s):
        here, mine, part = spots(t - steps - 1, s)
        v = line_ref[(t - steps - 1) * SUB + s]
        slot = jnp.where(v >= 1024.0, v - 1024.0, v)
        xt_ref[0:D, part] = jnp.transpose(edge_ref[part, :])
        line = lax.broadcasted_iota(jnp.int32, (D, rows), 0).astype(F32).astype(BF16)
        for block in range(table // D):
            wanted = (slot - float(block * D)).astype(BF16)
            xt_ref[D + block * D : 2 * D + block * D, part] = jnp.where(
                line == wanted, jnp.ones((), BF16), jnp.zeros((), BF16)
            )
        cot = ecot_ref[part, :].astype(F32)
        base = pl.multiple_of((t - steps - 1) * (R * SUB) + s * R, R)
        dx = (cot + spread_rows(dgath_ref, base)) * g_e[...]
        normed = xh_ref[here, :].astype(F32)
        share_of = jnp.mean(dx * normed, 1, keepdims=True)
        dz = (rm_ref[here, :] * (dx - normed * share_of)).astype(BF16)
        dz_ref[part, :] = dz
        dpre = (dot(dz, weot_ref[...]) * dsil_ref[here, :].astype(F32)).astype(BF16)
        dpre_ref[part, :] = dpre
        egrad_ref[part, :] = (cot + dot(dpre, wet_ref[...])).astype(BF16)
        egrad_copy(t - steps - 1, s).start()
        gd_ref[mine, :] = dot(g_ref[...], dpre).astype(BF16)

    @pl.when(t > steps + 1)
    def _():
        for s in range(SUB):
            egrad_copy(t - steps - 2, s).wait()

    @pl.when(t > steps)
    def _():
        for s in range(SUB):
            third_half(s)
        span = pl.ds(pl.multiple_of((t - steps - 1) * (rows * SUB), rows), rows * SUB)
        gout_ref[...] += dot_rows(hid_ref[span, :], dz_ref[...])
        acc_ref[...] += dot(xt_ref[...], dpre_ref[...])

    @pl.when(t == 2 * steps)
    def _():
        own = own_ref[...]
        near = acc_ref[D : D + n, :].astype(BF16)
        far = acc_ref[D + n : seg, :].astype(BF16)
        wst = flipped(w_ein[D : 2 * D, :])
        back_ref[...] = dot(far, wst).astype(BF16).reshape(back_ref.shape)
        back_copy.start()
        gd = gd_ref[...]
        down_ref[...] += dot(near, wst) + dot(gd, flipped(w_ein[2 * D :, :]))
        down_copy.start()
        g_s = dot_rows(own, near) + dot_rows(far_ref[...], far)
        g_r = dot_rows(own, gd)
        whole = [acc_ref[0:D, :], g_s, g_r, centred(gout_ref[...])]
        whole += [gnode_ref[i * D : (i + 1) * D, :] for i in range(3)]
        at = 0
        for piece in whole:
            for i in range(D // 16):
                for j in range(2):
                    grads_ref[at] = piece[16 * i : 16 * i + 16, 128 * j : 128 * j + 128].astype(BF16)
                    at += 1
        for s in range(SUB):
            egrad_copy(steps - 1, s).wait()
        for copy in (nnew_copy, down_copy, back_copy):
            copy.wait()


def layer_call(node, far, near, edge, slot, mask, w_ein, w_eout, g_e, w_nin, b_n, w_nout, g_n, ncot, ecot):
    n, d = node.shape
    slots = slot.shape[0]
    rows = R * slots
    tiles = n // (R * SUB)
    table = n + far.shape[0]
    seg = d + table
    total = n * slots
    whole = pl.BlockSpec(memory_space=pltpu.VMEM)
    there = pl.BlockSpec(memory_space=pl.ANY)
    stream_e = pl.BlockSpec((rows * SUB, d), lambda t: (jnp.where(t < tiles, t, jnp.maximum(t - tiles - 1, 0)), 0))
    first = pl.BlockSpec((rows * SUB, d), lambda t: (jnp.minimum(t, tiles - 1), 0))
    second = pl.BlockSpec((rows * SUB, d), lambda t: (jnp.maximum(t - tiles - 1, 0), 0))
    tiles_all = 7 * (d // 16) * (d // 128)
    flops = 2 * total * d * (d * 8 + 2 * table)
    return pl.pallas_call(
        functools.partial(layer_kernel, tiles, slots),
        grid=(2 * tiles + 1,),
        in_specs=[whole, whole, first, stream_e] + [whole] * 5 + [there, whole, there, whole, there, second],
        out_specs=[there, first, there, there, there, whole],
        out_shape=[
            jax.ShapeDtypeStruct((n, d), BF16),
            jax.ShapeDtypeStruct((total, d), BF16),
            jax.ShapeDtypeStruct((total, d), BF16),
            jax.ShapeDtypeStruct((n, d), F32),
            jax.ShapeDtypeStruct((8, far.shape[0] // 8, d), BF16),
            jax.ShapeDtypeStruct((tiles_all, 16, 128), BF16),
        ],
        scratch_shapes=[
            pltpu.VMEM((SUB, rows, table - n), BF16),
            pltpu.VMEM((seg, SUB * rows), BF16),
            pltpu.VMEM((R, rows), BF16),
            pltpu.VMEM((SUB * rows, d), BF16),
            pltpu.VMEM((SUB * rows, d), BF16),
            pltpu.VMEM((table - n, d), BF16),
            pltpu.VMEM((d, d), BF16),
            pltpu.VMEM((d, d), BF16),
            pltpu.VMEM((d, d), BF16),
            pltpu.VMEM((n, 128), F32),
            pltpu.VMEM((32, n), BF16),
            pltpu.VMEM((128, n), F32),
            pltpu.VMEM((rows, 128), F32),
            pltpu.VMEM((n // R, 1, rows), F32),
            pltpu.VMEM((total, d), BF16),
            pltpu.VMEM((total, d), BF16),
            pltpu.VMEM((total, d), BF16),
            pltpu.VMEM((total, 1), F32),
            pltpu.VMEM((n, d), BF16),
            pltpu.VMEM((n, d), F32),
            pltpu.VMEM((seg, d), F32),
            pltpu.VMEM((d, d), F32),
            pltpu.VMEM((n, d), BF16),
            pltpu.VMEM((n, d), F32),
            pltpu.VMEM((3 * d, d), F32),
            pltpu.VMEM((SUB * rows, d), BF16),
            pltpu.VMEM((2 * d, d), BF16),
            pltpu.VMEM((d, d), BF16),
            pltpu.VMEM((n, d), BF16),
            pltpu.VMEM((n, d), BF16),
            pltpu.VMEM((8, far.shape[0] // 8, d), BF16),
            pltpu.SemaphoreType.DMA((SUB,)),
            pltpu.SemaphoreType.DMA((6,)),
        ],
        compiler_params=pltpu.CompilerParams(vmem_limit_bytes=60 * 1024 * 1024),
        cost_estimate=pl.CostEstimate(flops=flops, bytes_accessed=5 * total * d * 2, transcendentals=total * d),
    )(node, far, near, edge, slot, mask, w_ein, w_eout, g_e.reshape(1, -1), w_nin, b_n.reshape(1, -1), w_nout, g_n.reshape(1, -1), ncot, ecot)


band_steps = (-1, -1, -1, 0, 0, 1, 1, 1)
sector_steps = (-1, 0, 1, -1, 1, -1, 0, 1)
MESH = pl.DeviceIdType.MESH


def neighbours(bands, sectors):
    band, sector = lax.axis_index("band"), lax.axis_index("sector")
    ahead = [
        (lax.rem(band + b + bands, bands), lax.rem(sector + s + sectors, sectors))
        for b, s in zip(band_steps, sector_steps)
    ]
    return ahead


def picked(wanted, count):
    line = lax.broadcasted_iota(jnp.int32, (count, wanted.shape[1]), 0)
    return jnp.where(line == wanted, 1.0, 0.0).astype(BF16)


def fetch_kernel(
    bands, sectors, slots, node_hbm, rows_ref, slot_ref, w_ein, b_e, edge_ref, far_ref, near_ref,
    out_ref, node_ref, wcat_ref, recv_ref, value_ref, flip_ref, sel_ref, x_ref,
    send_sem, recv_sem, load_sem,
):
    t = pl.program_id(0)
    ahead = neighbours(bands, sectors)
    rows = R * slots
    n = node_ref.shape[0]
    copies = [
        pltpu.make_async_remote_copy(
            src_ref=out_ref.at[j],
            dst_ref=far_ref.at[j],
            send_sem=send_sem.at[j],
            recv_sem=recv_sem.at[j],
            device_id=ahead[7 - j],
            device_id_type=MESH,
        )
        for j in range(8)
    ]

    @pl.when(t == 0)
    def _():
        barrier = pltpu.get_barrier_semaphore()
        for place in ahead:
            pl.semaphore_signal(barrier, inc=1, device_id=place, device_id_type=MESH)
        load = pltpu.make_async_copy(node_hbm, node_ref, load_sem)
        load.start()
        load.wait()
        node = node_ref[...]
        for j in range(8):
            choice = picked(rows_ref[0, j : j + 1, :], n)
            out_ref[j] = dot_rows(choice, node).astype(BF16)
        pl.semaphore_wait(barrier, 8)
        for copy in copies:
            copy.start()
        wcat_ref[0:D, :] = w_ein[0:D, :]
        wcat_ref[D : D + n, :] = dot(node, w_ein[D : 2 * D, :]).astype(BF16)
        recv_ref[...] = dot(node, w_ein[2 * D :, :]) + b_e[...]
        flip_ref[...] = jnp.zeros_like(flip_ref)
        flip_ref[0:slots, :] = slot_ref[...].astype(F32)
        value_ref[...] = jnp.transpose(flip_ref[...])
        sel_ref[...] = slot_lanes(rows, slots)

    for s in range(SUB):
        base = pl.multiple_of(t * (R * SUB) + s * R, R)
        x = x_ref.at[s]
        x[:, 0:D] = edge_ref[s * rows : (s + 1) * rows, :]
        slot = jnp.sum(spread_rows(value_ref, base) * sel_ref[...], 1, keepdims=True)
        lane = lax.broadcasted_iota(jnp.int32, (rows, D), 1).astype(F32).astype(BF16)
        for block in range(n // D):
            wanted = (slot - float(block * D)).astype(BF16)
            x[:, D + block * D : 2 * D + block * D] = jnp.where(
                lane == wanted, jnp.ones((), BF16), jnp.zeros((), BF16)
            )
        near = dot(x[...], wcat_ref[...]) + spread_rows(recv_ref, base)
        near_ref[s * rows : (s + 1) * rows, :] = near.astype(BF16)

    @pl.when(t == pl.num_programs(0) - 1)
    def _():
        for copy in copies:
            copy.wait()


def fetch_call(bands, sectors, node, rows_in, slot, w_ein, b_e, edge):
    cap, (n, d) = rows_in.shape[2], node.shape
    slots = slot.shape[0]
    rows = R * slots
    whole = pl.BlockSpec(memory_space=pltpu.VMEM)
    there = pl.BlockSpec(memory_space=pl.ANY)
    stream = pl.BlockSpec((rows * SUB, d), lambda t: (t, 0))
    return pl.pallas_call(
        functools.partial(fetch_kernel, bands, sectors, slots),
        grid=(n // (R * SUB),),
        in_specs=[there, whole, whole, whole, whole, stream],
        out_specs=[there, stream],
        out_shape=[
            jax.ShapeDtypeStruct((8, cap, d), BF16),
            jax.ShapeDtypeStruct(edge.shape, BF16),
        ],
        scratch_shapes=[
            pltpu.VMEM((8, cap, d), BF16),
            pltpu.VMEM((n, d), BF16),
            pltpu.VMEM((d + n, d), BF16),
            pltpu.VMEM((n, d), F32),
            pltpu.VMEM((n, 128), F32),
            pltpu.VMEM((128, n), F32),
            pltpu.VMEM((rows, 128), F32),
            pltpu.VMEM((SUB, rows, d + n), BF16),
            pltpu.SemaphoreType.DMA((8,)),
            pltpu.SemaphoreType.DMA((8,)),
            pltpu.SemaphoreType.DMA,
        ],
        compiler_params=pltpu.CompilerParams(
            collective_id=0, has_side_effects=True, vmem_limit_bytes=60 * 1024 * 1024
        ),
    )(node, rows_in, slot, w_ein, b_e.reshape(1, -1), edge)


def sum_kernel(
    bands, sectors, share, back_ref, grads_ref, arrived_ref, out_ref,
    half_ref, one_ref, two_ref, three_ref, first_in, second_in, third_in,
    mine_ref, send_sem, recv_sem, core_sem, back_send, back_recv, load_sem,
):
    ahead = neighbours(bands, sectors)
    band, sector = lax.axis_index("band"), lax.axis_index("sector")
    core = lax.rem(band, 2)
    x = lax.rem(band // 2, 4)
    z = band // 8
    at = {"x": x, "y": sector, "z": z}

    def place(axis, index):
        if axis == "x":
            return ((z * 4 + index) * 2 + core, sector)
        if axis == "z":
            return ((index * 4 + x) * 2 + core, sector)
        return (band, index)

    def others(axis):
        return [lax.rem(at[axis] + i, 4) for i in (1, 2, 3)]

    sibling = (band + 1 - 2 * core, sector)
    peers = [place("x", i) for i in others("x")] + [place("z", i) for i in others("z")]
    peers += [place("y", lax.rem(sector + 2, 4))]
    barrier = pltpu.get_barrier_semaphore()
    for spot in ahead + peers:
        pl.semaphore_signal(barrier, inc=1, device_id=spot, device_id_type=MESH)
    load = pltpu.make_async_copy(grads_ref.at[core], mine_ref, load_sem)
    load.start()
    pl.semaphore_wait(barrier, len(ahead + peers))

    returns = []
    core_copy = pltpu.make_async_remote_copy(
        src_ref=grads_ref.at[1 - core], dst_ref=half_ref,
        send_sem=core_sem.at[0], recv_sem=core_sem.at[1],
        device_id=sibling, device_id_type=MESH,
    )
    core_copy.start()
    for j in range(8):
        returns.append(
            pltpu.make_async_remote_copy(
                src_ref=back_ref.at[j], dst_ref=arrived_ref.at[j],
                send_sem=back_send.at[j], recv_sem=back_recv.at[j],
                device_id=ahead[j], device_id_type=MESH,
            )
        )
        returns[-1].start()

    orders = (("x", "y", "z"), ("y", "z", "x"), ("z", "x", "y"))
    starts = [16 * sum(share[:p]) for p in range(3)]

    def exchange(stage, p, axis, source, target):
        copies = []
        for i, other in enumerate(others(axis)):
            copies.append(
                pltpu.make_async_remote_copy(
                    src_ref=source(other, i), dst_ref=target(i),
                    send_sem=send_sem.at[stage, p, i], recv_sem=recv_sem.at[stage, p, i],
                    device_id=place(axis, other), device_id_type=MESH,
                )
            )
            copies[-1].start()
        return copies

    def finish(copies):
        for copy in copies:
            copy.wait()

    load.wait()
    core_copy.wait()
    one_ref[...] = (mine_ref[...].astype(F32) + half_ref[...].astype(F32)).astype(BF16)

    live = []
    for p in range(3):
        m, axis = share[p], orders[p][0]
        live.append(exchange(
            0, p, axis,
            lambda other, i, p=p, m=m: one_ref.at[pl.ds(starts[p] + other * (4 * m), 4 * m)],
            lambda i, p=p, m=m: first_in.at[i, pl.ds(4 * sum(share[:p]), 4 * m)],
        ))
    for p in range(3):
        m, axis, low = share[p], orders[p][0], 4 * sum(share[:p])
        finish(live[p])
        total = one_ref[pl.ds(starts[p] + at[axis] * (4 * m), 4 * m)].astype(F32)
        for i in range(3):
            total += first_in[i, low : low + 4 * m].astype(F32)
        two_ref[low : low + 4 * m] = total.astype(BF16)
        live[p] = exchange(
            1, p, orders[p][1],
            lambda other, i, low=low, m=m: two_ref.at[pl.ds(low + other * m, m)],
            lambda i, p=p, m=m: second_in.at[i, pl.ds(sum(share[:p]), m)],
        )
    for p in range(3):
        m, axis, low, mid = share[p], orders[p][1], sum(share[:p]), 4 * sum(share[:p])
        finish(live[p])
        total = two_ref[pl.ds(mid + at[axis] * m, m)].astype(F32)
        for i in range(3):
            total += second_in[i, low : low + m].astype(F32)
        three_ref[low : low + m] = total.astype(BF16)
        third = orders[p][2]
        third_in[at[third], low : low + m] = total.astype(BF16)
        live[p] = exchange(
            2, p, third,
            lambda other, i, low=low, m=m: three_ref.at[pl.ds(low, m)],
            lambda i, low=low, m=m, third=third: third_in.at[at[third], pl.ds(low, m)],
        )
    for p in range(3):
        m, low = share[p], sum(share[:p])
        finish(live[p])
        total = third_in[0, low : low + m].astype(F32)
        for i in range(1, 4):
            total += third_in[i, low : low + m].astype(F32)
        spot = starts[p] + at[orders[p][0]] * (4 * m) + at[orders[p][1]] * m
        out_ref[core, pl.ds(spot, m)] = total.astype(BF16)
        live[p] = exchange(
            3, p, orders[p][1],
            lambda other, i, spot=spot, m=m: out_ref.at[core, pl.ds(spot, m)],
            lambda i, spot=spot, m=m: out_ref.at[core, pl.ds(spot, m)],
        )
    for p in range(3):
        m = share[p]
        finish(live[p])
        spot = starts[p] + at[orders[p][0]] * (4 * m)
        live[p] = exchange(
            4, p, orders[p][0],
            lambda other, i, spot=spot, m=m: out_ref.at[core, pl.ds(spot, 4 * m)],
            lambda i, spot=spot, m=m: out_ref.at[core, pl.ds(spot, 4 * m)],
        )
    last = []
    for p in range(3):
        finish(live[p])
        spot, m = starts[p], 16 * share[p]
        last.append(pltpu.make_async_remote_copy(
            src_ref=out_ref.at[core, pl.ds(spot, m)], dst_ref=out_ref.at[core, pl.ds(spot, m)],
            send_sem=core_sem.at[2 + p], recv_sem=core_sem.at[5 + p],
            device_id=sibling, device_id_type=MESH,
        ))
        last[-1].start()
    finish(returns)
    finish(last)


def sum_call(bands, sectors, back, grads):
    half = grads.shape[0] // 2
    unit = half // 16
    share = (unit - 2 * (unit // 3), unit // 3, unit // 3)
    whole = pl.BlockSpec(memory_space=pltpu.VMEM)
    there = pl.BlockSpec(memory_space=pl.ANY)
    tile = grads.shape[1:]
    return pl.pallas_call(
        functools.partial(sum_kernel, bands, sectors, share),
        in_specs=[there, there],
        out_specs=[there, whole],
        out_shape=[
            jax.ShapeDtypeStruct(back.shape, BF16),
            jax.ShapeDtypeStruct((2, half) + tile, BF16),
        ],
        scratch_shapes=[
            pltpu.VMEM((half,) + tile, BF16),
            pltpu.VMEM((half,) + tile, BF16),
            pltpu.VMEM((half // 4,) + tile, BF16),
            pltpu.VMEM((unit,) + tile, BF16),
            pltpu.VMEM((3, half // 4) + tile, BF16),
            pltpu.VMEM((3, unit) + tile, BF16),
            pltpu.VMEM((4, unit) + tile, BF16),
            pltpu.VMEM((half,) + tile, BF16),
            pltpu.SemaphoreType.DMA((5, 3, 3)),
            pltpu.SemaphoreType.DMA((5, 3, 3)),
            pltpu.SemaphoreType.DMA((8,)),
            pltpu.SemaphoreType.DMA((8,)),
            pltpu.SemaphoreType.DMA((8,)),
            pltpu.SemaphoreType.DMA,
        ],
        compiler_params=pltpu.CompilerParams(
            collective_id=1, has_side_effects=True, vmem_limit_bytes=60 * 1024 * 1024
        ),
    )(back, grads.reshape((2, half) + tile))


def close_kernel(scale, rows_ref, arrived_hbm, part_hbm, sums_hbm, *refs):
    targets, (arrived_ref, part_ref, sums_ref, ngrad_ref), outs = refs[:5], refs[5:9], refs[9:13]
    load_sem, store_sem = refs[13:]
    spans, at = [], 0
    for out in outs:
        size = out.shape[0] // 8
        spans.append((at, size))
        at += size
    loads = [
        pltpu.make_async_copy(sums_hbm.at[start : start + size], sums_ref.at[start : start + size], load_sem.at[i])
        for i, (start, size) in enumerate(spans)
    ]
    loads.append(pltpu.make_async_copy(part_hbm, part_ref, load_sem.at[4]))
    loads.append(pltpu.make_async_copy(arrived_hbm, arrived_ref, load_sem.at[5]))
    for load in loads:
        load.start()
    stores = [
        pltpu.make_async_copy(ref, target, store_sem.at[i])
        for i, (ref, target) in enumerate(zip(outs + (ngrad_ref,), targets[1:] + targets[:1]))
    ]
    n = part_ref.shape[0]
    chosen = [picked(rows_ref[0, j : j + 1, :], n) for j in range(8)]
    for i, (out, (start, size)) in enumerate(zip(outs, spans)):
        loads[i].wait()
        for tile in range(size):
            r, l = 16 * (tile // 2), 128 * (tile % 2)
            out[r : r + 16, l : l + 128] = sums_ref[start + tile].astype(F32) * scale
        stores[i].start()
    loads[4].wait()
    loads[5].wait()
    total = part_ref[...]
    for j in range(8):
        total += dot(chosen[j], arrived_ref[j])
    ngrad_ref[...] = total
    stores[4].start()
    for store in stores:
        store.wait()


def close_call(scale, rows, arrived, part, sums):
    d = part.shape[1]
    whole = pl.BlockSpec(memory_space=pltpu.VMEM)
    there = pl.BlockSpec(memory_space=pl.ANY)
    outs = [part.shape, (3 * d, d), (d, d), (2 * d, d), (d, d)]
    sums = sums.reshape((-1,) + sums.shape[2:])
    return pl.pallas_call(
        functools.partial(close_kernel, scale),
        in_specs=[whole, there, there, there],
        out_specs=[there] * 5,
        out_shape=[jax.ShapeDtypeStruct(shape, F32) for shape in outs],
        scratch_shapes=[
            pltpu.VMEM(arrived.shape, BF16),
            pltpu.VMEM(part.shape, F32),
            pltpu.VMEM(sums.shape, BF16),
        ]
        + [pltpu.VMEM(shape, F32) for shape in outs]
        + [pltpu.SemaphoreType.DMA((6,)), pltpu.SemaphoreType.DMA((5,))],
        compiler_params=pltpu.CompilerParams(vmem_limit_bytes=60 * 1024 * 1024),
    )(rows, arrived, part, sums)


def solution(mesh):
    bands, sectors = mesh.shape["band"], mesh.shape["sector"]

    def local(node, edge, slot, mask, rows, w_ein, b_e, w_eout, g_e, w_nin, b_n, w_nout, g_n, ncot, ecot):
        n, d = node.shape
        slot_t, mask_t = slot.T, mask.T
        far, near = fetch_call(bands, sectors, node, rows, slot_t, w_ein, b_e, edge)
        nnew, enew, egrad, part, back, grads = layer_call(
            node, far.reshape(-1, d), near, edge, slot_t, mask_t,
            w_ein, w_eout, g_e, w_nin, b_n, w_nout, g_n, ncot, ecot,
        )
        arrived, sums = sum_call(bands, sectors, back, grads)
        scale = float(bands * sectors * n * slot.shape[1]) ** (-0.5)
        outs = close_call(scale, rows, arrived, part, sums)
        return (nnew, enew, outs[0], egrad) + tuple(outs[1:])

    split = P(("band", "sector"), None)
    in_specs = (split,) * 4 + (P(("band", "sector"), None, None),) + (P(),) * 8 + (split, split)
    out_specs = (split,) * 4 + (P(),) * 4
    return jax.shard_map(local, mesh=mesh, in_specs=in_specs, out_specs=out_specs, check_vma=False)
```

```python
import functools
import jax
import jax.numpy as jnp
from jax import lax
from jax.experimental import pallas as pl
from jax.experimental.pallas import tpu as pltpu
from jax.sharding import PartitionSpec as P

F32, BF16 = jnp.float32, jnp.bfloat16
R = 64
SUB = 4
D = 256


def dot(a, b):
    return jnp.dot(a, b, preferred_element_type=F32)


def dot_rows(a, b):
    return lax.dot_general(a, b, (((0,), (0,)), ((), ())), preferred_element_type=F32)


def silu_parts(pre):
    gate = 0.5 * jnp.tanh(0.5 * pre) + 0.5
    hidden = pre * gate
    return hidden, gate + hidden * (1.0 - gate)


def centred(matrix):
    return matrix - jnp.mean(matrix, 1, keepdims=True)


def flipped(matrix):
    return jnp.transpose(matrix.astype(F32)).astype(BF16)


def layer_kernel(
    steps, slots,
    own_ref, far_ref, edge_ref, slot_ref, mask_ref,
    w_ein, b_e, w_eout, g_e, nin_hbm, b_n, nout_hbm, g_n, ncot_hbm, ecot_ref,
    nnew_hbm, enew_ref, egrad_hbm, ngrad_hbm, back_hbm, grads_ref,
    x_ref, xt_ref, g_ref, dz_ref, dpre_ref, wcat_ref, weo_ref, weot_ref, wet_ref, recv_ref, value_ref, parts_ref, partst_ref,
    sel_ref, line_ref, hid_ref, dsil_ref, xh_ref, rm_ref, gath_ref, dgath_ref,
    acc_ref, gout_ref, gd_ref, down_ref, gnode_ref,
    egrad_ref, w_nin, w_nout, ncot_ref, nnew_ref, back_ref, egrad_sem, node_sem,
):
    t = pl.program_id(0)
    rows = R * slots
    n = own_ref.shape[0]
    table = n + far_ref.shape[0]
    seg = D + table

    def spread_rows(ref, base):
        upper = lax.broadcasted_iota(jnp.int32, (8, ref.shape[1]), 0) < 4
        pieces = []
        for pair in range(R // 2):
            a = jnp.broadcast_to(ref[pl.ds(base + 2 * pair, 1), :], (8, ref.shape[1]))
            b = jnp.broadcast_to(ref[pl.ds(base + 2 * pair + 1, 1), :], (8, ref.shape[1]))
            pieces += [a, jnp.where(upper, a, b), b]
        return jnp.concatenate(pieces, axis=0)

    late = [
        pltpu.make_async_copy(nin_hbm, w_nin, node_sem.at[0]),
        pltpu.make_async_copy(nout_hbm, w_nout, node_sem.at[1]),
        pltpu.make_async_copy(ncot_hbm, ncot_ref, node_sem.at[2]),
    ]
    nnew_copy = pltpu.make_async_copy(nnew_ref, nnew_hbm, node_sem.at[3])
    down_copy = pltpu.make_async_copy(down_ref, ngrad_hbm, node_sem.at[4])
    back_copy = pltpu.make_async_copy(back_ref, back_hbm, node_sem.at[5])

    def egrad_copy(step, s):
        span = pl.ds(pl.multiple_of((step * SUB + s) * rows, rows), rows)
        return pltpu.make_async_copy(egrad_ref.at[s * rows : (s + 1) * rows, :], egrad_hbm.at[span, :], egrad_sem.at[s])

    @pl.when(t == 0)
    def _():
        for copy in late:
            copy.start()
        e = lax.broadcasted_iota(jnp.int32, (R, rows), 1)
        r = lax.broadcasted_iota(jnp.int32, (R, rows), 0)
        gap = e - slots * r
        inside = (gap >= 0) & (gap < slots)
        g_ref[...] = jnp.where(inside, 1.0, 0.0).astype(BF16)
        ef = lax.broadcasted_iota(jnp.int32, (32, rows), 1).astype(F32)
        lf = lax.broadcasted_iota(jnp.int32, (32, rows), 0).astype(F32)
        k = ef - slots * jnp.floor((ef + 0.5) * (1.0 / slots))
        selt = jnp.where(lf == k, 32.0, 0.0) + jnp.where(lf == k + 16.0, 1.0, 0.0)
        ef = lax.broadcasted_iota(jnp.int32, (rows, 128), 0).astype(F32)
        lf = lax.broadcasted_iota(jnp.int32, (rows, 128), 1).astype(F32)
        k = ef - slots * jnp.floor((ef + 0.5) * (1.0 / slots))
        sel_ref[...] = jnp.where(lf == k, 1.0, 0.0)
        v = slot_ref[...] + 1024 * mask_ref[...]
        partst_ref[...] = jnp.zeros_like(partst_ref)
        partst_ref[0:slots, :] = v.astype(F32)
        value_ref[...] = jnp.transpose(partst_ref[...])
        high = (v >> 5).astype(F32)
        low = (v & 31).astype(F32)
        parts_ref[...] = jnp.zeros_like(parts_ref)
        parts_ref[0:16, :] = jnp.concatenate([high, jnp.zeros((16 - slots, n), F32)], axis=0).astype(BF16)
        parts_ref[16:32, :] = jnp.concatenate([low, jnp.zeros((16 - slots, n), F32)], axis=0).astype(BF16)
        for tile in range(n // R):
            piece = dot(parts_ref[0:32, tile * R : tile * R + R], g_ref[...])
            line_ref[tile] = jnp.sum(piece * selt, 0, keepdims=True)
        wcat_ref[0:D, :] = w_ein[0:D, :]
        wcat_ref[D : D + n, :] = dot(own_ref[...], w_ein[D : 2 * D, :]).astype(BF16)
        wcat_ref[D + n : seg, :] = dot(far_ref[...], w_ein[D : 2 * D, :]).astype(BF16)
        recv_ref[...] = dot(own_ref[...], w_ein[2 * D :, :]) + b_e[...]
        weo = centred(w_eout[...].astype(F32))
        weo_ref[...] = weo.astype(BF16)
        weot_ref[...] = jnp.transpose(weo).astype(BF16)
        wet_ref[...] = flipped(w_ein[0:D, :])
        acc_ref[...] = jnp.zeros_like(acc_ref)
        gout_ref[...] = jnp.zeros_like(gout_ref)

    def spots(step, s):
        at = step * (R * SUB) + s * R
        here = pl.ds(pl.multiple_of(at * slots, rows), rows)
        mine = pl.ds(pl.multiple_of(at, R), R)
        return here, mine, slice(s * rows, (s + 1) * rows)

    def first_half(s):
        here, mine, part = spots(t, s)
        x = x_ref.at[s]
        x[:, 0:D] = edge_ref[part, :]
        base = pl.multiple_of(t * (R * SUB) + s * R, R)
        v = jnp.sum(spread_rows(value_ref, base) * sel_ref[...], 1, keepdims=True)
        real = v >= 1024.0
        slot = jnp.where(real, v - 1024.0, v)
        lane = lax.broadcasted_iota(jnp.int32, (rows, D), 1).astype(F32).astype(BF16)
        for block in range(table // D):
            wanted = (slot - float(block * D)).astype(BF16)
            x[:, D + block * D : 2 * D + block * D] = jnp.where(
                lane == wanted, jnp.ones((), BF16), jnp.zeros((), BF16)
            )
        pre = dot(x[...], wcat_ref[...]) + spread_rows(recv_ref, base)
        return pre, jnp.where(real, 1.0, 0.0)

    def second_half(s, pre, keep):
        here, mine, part = spots(t, s)
        hidden, slope = silu_parts(pre)
        hidden = hidden.astype(BF16)
        hid_ref[here, :] = hidden
        dsil_ref[here, :] = slope.astype(BF16)
        c = dot(hidden, weo_ref[...])
        rstd = lax.rsqrt(jnp.mean(c * c, 1, keepdims=True) + 1e-05)
        kept = rstd * keep
        normed = c * kept
        xh_ref[here, :] = normed.astype(BF16)
        rm_ref[here, :] = kept
        update = normed * g_e[...]
        enew_ref[part, :] = (edge_ref[part, :].astype(F32) + update).astype(BF16)
        gath_ref[mine, :] = dot(g_ref[...], update.astype(BF16)).astype(BF16)

    @pl.when(t < steps)
    def _():
        held = first_half(0)
        for s in range(1, SUB):
            following = first_half(s)
            second_half(s - 1, *held)
            held = following
        second_half(SUB - 1, *held)

    @pl.when(t == steps)
    def _():
        for copy in late:
            copy.wait()
        own = own_ref[...]
        gath = gath_ref[...]
        pre = dot(own, w_nin[0:D, :]) + dot(gath, w_nin[D:, :]) + b_n[...]
        hidden, slope = silu_parts(pre)
        hidden = hidden.astype(BF16)
        wno = centred(w_nout[...].astype(F32))
        c = dot(hidden, wno.astype(BF16))
        rstd = lax.rsqrt(jnp.mean(c * c, 1, keepdims=True) + 1e-05)
        normed = c * rstd
        nnew_ref[...] = (own.astype(F32) + normed * g_n[...]).astype(BF16)
        nnew_copy.start()
        cot = ncot_ref[...].astype(F32)
        dx = cot * g_n[...]
        share = jnp.mean(dx * normed, 1, keepdims=True)
        dz = (rstd * (dx - normed * share)).astype(BF16)
        gnode_ref[2 * D : 3 * D, :] = centred(dot_rows(hidden, dz))
        dpre = (dot(dz, jnp.transpose(wno).astype(BF16)) * slope).astype(BF16)
        gnode_ref[0:D, :] = dot_rows(own, dpre)
        gnode_ref[D : 2 * D, :] = dot_rows(gath, dpre)
        down_ref[...] = cot + dot(dpre, flipped(w_nin[0:D, :]))
        dgath_ref[...] = dot(dpre, flipped(w_nin[D:, :]))

    def third_half(s):
        here, mine, part = spots(t - steps - 1, s)
        v = line_ref[(t - steps - 1) * SUB + s]
        slot = jnp.where(v >= 1024.0, v - 1024.0, v)
        xt_ref[0:D, part] = jnp.transpose(edge_ref[part, :])
        line = lax.broadcasted_iota(jnp.int32, (D, rows), 0).astype(F32).astype(BF16)
        for block in range(table // D):
            wanted = (slot - float(block * D)).astype(BF16)
            xt_ref[D + block * D : 2 * D + block * D, part] = jnp.where(
                line == wanted, jnp.ones((), BF16), jnp.zeros((), BF16)
            )
        cot = ecot_ref[part, :].astype(F32)
        base = pl.multiple_of((t - steps - 1) * (R * SUB) + s * R, R)
        dx = (cot + spread_rows(dgath_ref, base)) * g_e[...]
        normed = xh_ref[here, :].astype(F32)
        share_of = jnp.mean(dx * normed, 1, keepdims=True)
        dz = (rm_ref[here, :] * (dx - normed * share_of)).astype(BF16)
        dz_ref[part, :] = dz
        return cot, dz

    def final_half(s, cot, dz):
        here, mine, part = spots(t - steps - 1, s)
        dpre = (dot(dz, weot_ref[...]) * dsil_ref[here, :].astype(F32)).astype(BF16)
        dpre_ref[part, :] = dpre
        egrad_ref[part, :] = (cot + dot(dpre, wet_ref[...])).astype(BF16)
        egrad_copy(t - steps - 1, s).start()
        gd_ref[mine, :] = dot(g_ref[...], dpre).astype(BF16)

    @pl.when(t > steps + 1)
    def _():
        for s in range(SUB):
            egrad_copy(t - steps - 2, s).wait()

    @pl.when(t > steps)
    def _():
        held = third_half(0)
        for s in range(1, SUB):
            following = third_half(s)
            final_half(s - 1, *held)
            held = following
        final_half(SUB - 1, *held)
        span = pl.ds(pl.multiple_of((t - steps - 1) * (rows * SUB), rows), rows * SUB)
        gout_ref[...] += dot_rows(hid_ref[span, :], dz_ref[...])
        acc_ref[...] += dot(xt_ref[...], dpre_ref[...])

    @pl.when(t == 2 * steps)
    def _():
        own = own_ref[...]
        near = acc_ref[D : D + n, :].astype(BF16)
        far = acc_ref[D + n : seg, :].astype(BF16)
        wst = flipped(w_ein[D : 2 * D, :])
        back_ref[...] = dot(far, wst).astype(BF16).reshape(back_ref.shape)
        back_copy.start()
        gd = gd_ref[...]
        down_ref[...] += dot(near, wst) + dot(gd, flipped(w_ein[2 * D :, :]))
        down_copy.start()
        g_s = dot_rows(own, near) + dot_rows(far_ref[...], far)
        g_r = dot_rows(own, gd)
        whole = [acc_ref[0:D, :], g_s, g_r, centred(gout_ref[...])]
        whole += [gnode_ref[i * D : (i + 1) * D, :] for i in range(3)]
        at = 0
        for piece in whole:
            for i in range(D // 16):
                for j in range(2):
                    grads_ref[at] = piece[16 * i : 16 * i + 16, 128 * j : 128 * j + 128].astype(BF16)
                    at += 1
        for s in range(SUB):
            egrad_copy(steps - 1, s).wait()
        for copy in (nnew_copy, down_copy, back_copy):
            copy.wait()


def layer_call(node, far, edge, slot, mask, w_ein, b_e, w_eout, g_e, w_nin, b_n, w_nout, g_n, ncot, ecot):
    n, d = node.shape
    slots = slot.shape[1]
    rows = R * slots
    tiles = n // (R * SUB)
    table = n + far.shape[0]
    seg = d + table
    total = n * slots
    whole = pl.BlockSpec(memory_space=pltpu.VMEM)
    there = pl.BlockSpec(memory_space=pl.ANY)
    stream_e = pl.BlockSpec((rows * SUB, d), lambda t: (jnp.where(t < tiles, t, jnp.maximum(t - tiles - 1, 0)), 0))
    first = pl.BlockSpec((rows * SUB, d), lambda t: (jnp.minimum(t, tiles - 1), 0))
    second = pl.BlockSpec((rows * SUB, d), lambda t: (jnp.maximum(t - tiles - 1, 0), 0))
    tiles_all = 7 * (d // 16) * (d // 128)
    flops = 2 * total * d * (d * 8 + 2 * table)
    return pl.pallas_call(
        functools.partial(layer_kernel, tiles, slots),
        grid=(2 * tiles + 1,),
        in_specs=[whole, whole, stream_e] + [whole] * 6 + [there, whole, there, whole, there, second],
        out_specs=[there, first, there, there, there, whole],
        out_shape=[
            jax.ShapeDtypeStruct((n, d), BF16),
            jax.ShapeDtypeStruct((total, d), BF16),
            jax.ShapeDtypeStruct((total, d), BF16),
            jax.ShapeDtypeStruct((n, d), F32),
            jax.ShapeDtypeStruct((8, far.shape[0] // 8, d), BF16),
            jax.ShapeDtypeStruct((tiles_all, 16, 128), BF16),
        ],
        scratch_shapes=[
            pltpu.VMEM((SUB, rows, seg), BF16),
            pltpu.VMEM((seg, SUB * rows), BF16),
            pltpu.VMEM((R, rows), BF16),
            pltpu.VMEM((SUB * rows, d), BF16),
            pltpu.VMEM((SUB * rows, d), BF16),
            pltpu.VMEM((seg, d), BF16),
            pltpu.VMEM((d, d), BF16),
            pltpu.VMEM((d, d), BF16),
            pltpu.VMEM((d, d), BF16),
            pltpu.VMEM((n, d), F32),
            pltpu.VMEM((n, 128), F32),
            pltpu.VMEM((32, n), BF16),
            pltpu.VMEM((128, n), F32),
            pltpu.VMEM((rows, 128), F32),
            pltpu.VMEM((n // R, 1, rows), F32),
            pltpu.VMEM((total, d), BF16),
            pltpu.VMEM((total, d), BF16),
            pltpu.VMEM((total, d), BF16),
            pltpu.VMEM((total, 1), F32),
            pltpu.VMEM((n, d), BF16),
            pltpu.VMEM((n, d), F32),
            pltpu.VMEM((seg, d), F32),
            pltpu.VMEM((d, d), F32),
            pltpu.VMEM((n, d), BF16),
            pltpu.VMEM((n, d), F32),
            pltpu.VMEM((3 * d, d), F32),
            pltpu.VMEM((SUB * rows, d), BF16),
            pltpu.VMEM((2 * d, d), BF16),
            pltpu.VMEM((d, d), BF16),
            pltpu.VMEM((n, d), BF16),
            pltpu.VMEM((n, d), BF16),
            pltpu.VMEM((8, far.shape[0] // 8, d), BF16),
            pltpu.SemaphoreType.DMA((SUB,)),
            pltpu.SemaphoreType.DMA((6,)),
        ],
        compiler_params=pltpu.CompilerParams(vmem_limit_bytes=60 * 1024 * 1024),
        cost_estimate=pl.CostEstimate(flops=flops, bytes_accessed=5 * total * d * 2, transcendentals=total * d),
    )(node, far, edge, slot.T, mask.T, w_ein, b_e.reshape(1, -1), w_eout, g_e.reshape(1, -1), w_nin, b_n.reshape(1, -1), w_nout, g_n.reshape(1, -1), ncot, ecot)


band_steps = (-1, -1, -1, 0, 0, 1, 1, 1)
sector_steps = (-1, 0, 1, -1, 1, -1, 0, 1)
MESH = pl.DeviceIdType.MESH


def neighbours(bands, sectors):
    band, sector = lax.axis_index("band"), lax.axis_index("sector")
    ahead = [
        (lax.rem(band + b + bands, bands), lax.rem(sector + s + sectors, sectors))
        for b, s in zip(band_steps, sector_steps)
    ]
    return ahead


def picked(wanted, count):
    line = lax.broadcasted_iota(jnp.int32, (count, wanted.shape[1]), 0)
    return jnp.where(line == wanted, 1.0, 0.0).astype(BF16)


def fetch_kernel(
    bands, sectors, node_hbm, rows_ref, far_ref, out_ref, node_ref, send_sem, recv_sem, load_sem
):
    ahead = neighbours(bands, sectors)
    barrier = pltpu.get_barrier_semaphore()
    for place in ahead:
        pl.semaphore_signal(barrier, inc=1, device_id=place, device_id_type=MESH)
    load = pltpu.make_async_copy(node_hbm, node_ref, load_sem)
    load.start()
    load.wait()
    node = node_ref[...]
    for j in range(8):
        choice = picked(rows_ref[0, j : j + 1, :], node.shape[0])
        out_ref[j] = dot_rows(choice, node).astype(BF16)
    pl.semaphore_wait(barrier, 8)
    copies = []
    for j in range(8):
        copies.append(
            pltpu.make_async_remote_copy(
                src_ref=out_ref.at[j],
                dst_ref=far_ref.at[j],
                send_sem=send_sem.at[j],
                recv_sem=recv_sem.at[j],
                device_id=ahead[7 - j],
                device_id_type=MESH,
            )
        )
        copies[-1].start()
    for copy in copies:
        copy.wait()


def fetch_call(bands, sectors, node, rows):
    cap, d = rows.shape[2], node.shape[1]
    whole = pl.BlockSpec(memory_space=pltpu.VMEM)
    there = pl.BlockSpec(memory_space=pl.ANY)
    return pl.pallas_call(
        functools.partial(fetch_kernel, bands, sectors),
        in_specs=[there, whole],
        out_specs=there,
        out_shape=jax.ShapeDtypeStruct((8, cap, d), BF16),
        scratch_shapes=[
            pltpu.VMEM((8, cap, d), BF16),
            pltpu.VMEM(node.shape, BF16),
            pltpu.SemaphoreType.DMA((8,)),
            pltpu.SemaphoreType.DMA((8,)),
            pltpu.SemaphoreType.DMA,
        ],
        compiler_params=pltpu.CompilerParams(
            collective_id=0, has_side_effects=True, vmem_limit_bytes=60 * 1024 * 1024
        ),
    )(node, rows)


def sum_kernel(
    bands, sectors, share, back_ref, grads_ref, arrived_ref, out_ref,
    half_ref, one_ref, two_ref, three_ref, first_in, second_in, third_in,
    mine_ref, send_sem, recv_sem, core_sem, back_send, back_recv, load_sem,
):
    ahead = neighbours(bands, sectors)
    band, sector = lax.axis_index("band"), lax.axis_index("sector")
    core = lax.rem(band, 2)
    x = lax.rem(band // 2, 4)
    z = band // 8
    at = {"x": x, "y": sector, "z": z}

    def place(axis, index):
        if axis == "x":
            return ((z * 4 + index) * 2 + core, sector)
        if axis == "z":
            return ((index * 4 + x) * 2 + core, sector)
        return (band, index)

    def others(axis):
        return [lax.rem(at[axis] + i, 4) for i in (1, 2, 3)]

    sibling = (band + 1 - 2 * core, sector)
    peers = [place("x", i) for i in others("x")] + [place("z", i) for i in others("z")]
    peers += [place("y", lax.rem(sector + 2, 4))]
    barrier = pltpu.get_barrier_semaphore()
    for spot in ahead + peers:
        pl.semaphore_signal(barrier, inc=1, device_id=spot, device_id_type=MESH)
    load = pltpu.make_async_copy(grads_ref.at[core], mine_ref, load_sem)
    load.start()
    pl.semaphore_wait(barrier, len(ahead + peers))

    returns = []
    core_copy = pltpu.make_async_remote_copy(
        src_ref=grads_ref.at[1 - core], dst_ref=half_ref,
        send_sem=core_sem.at[0], recv_sem=core_sem.at[1],
        device_id=sibling, device_id_type=MESH,
    )
    core_copy.start()
    for j in range(8):
        returns.append(
            pltpu.make_async_remote_copy(
                src_ref=back_ref.at[j], dst_ref=arrived_ref.at[j],
                send_sem=back_send.at[j], recv_sem=back_recv.at[j],
                device_id=ahead[j], device_id_type=MESH,
            )
        )
        returns[-1].start()

    orders = (("x", "y", "z"), ("y", "z", "x"), ("z", "x", "y"))
    starts = [16 * sum(share[:p]) for p in range(3)]

    def exchange(stage, p, axis, source, target):
        copies = []
        for i, other in enumerate(others(axis)):
            copies.append(
                pltpu.make_async_remote_copy(
                    src_ref=source(other, i), dst_ref=target(i),
                    send_sem=send_sem.at[stage, p, i], recv_sem=recv_sem.at[stage, p, i],
                    device_id=place(axis, other), device_id_type=MESH,
                )
            )
            copies[-1].start()
        return copies

    def finish(copies):
        for copy in copies:
            copy.wait()

    load.wait()
    core_copy.wait()
    one_ref[...] = (mine_ref[...].astype(F32) + half_ref[...].astype(F32)).astype(BF16)

    live = []
    for p in range(3):
        m, axis = share[p], orders[p][0]
        live.append(exchange(
            0, p, axis,
            lambda other, i, p=p, m=m: one_ref.at[pl.ds(starts[p] + other * (4 * m), 4 * m)],
            lambda i, p=p, m=m: first_in.at[i, pl.ds(4 * sum(share[:p]), 4 * m)],
        ))
    for p in range(3):
        m, axis, low = share[p], orders[p][0], 4 * sum(share[:p])
        finish(live[p])
        total = one_ref[pl.ds(starts[p] + at[axis] * (4 * m), 4 * m)].astype(F32)
        for i in range(3):
            total += first_in[i, low : low + 4 * m].astype(F32)
        two_ref[low : low + 4 * m] = total.astype(BF16)
        live[p] = exchange(
            1, p, orders[p][1],
            lambda other, i, low=low, m=m: two_ref.at[pl.ds(low + other * m, m)],
            lambda i, p=p, m=m: second_in.at[i, pl.ds(sum(share[:p]), m)],
        )
    for p in range(3):
        m, axis, low, mid = share[p], orders[p][1], sum(share[:p]), 4 * sum(share[:p])
        finish(live[p])
        total = two_ref[pl.ds(mid + at[axis] * m, m)].astype(F32)
        for i in range(3):
            total += second_in[i, low : low + m].astype(F32)
        three_ref[low : low + m] = total.astype(BF16)
        third = orders[p][2]
        third_in[at[third], low : low + m] = total.astype(BF16)
        live[p] = exchange(
            2, p, third,
            lambda other, i, low=low, m=m: three_ref.at[pl.ds(low, m)],
            lambda i, low=low, m=m, third=third: third_in.at[at[third], pl.ds(low, m)],
        )
    for p in range(3):
        m, low = share[p], sum(share[:p])
        finish(live[p])
        total = third_in[0, low : low + m].astype(F32)
        for i in range(1, 4):
            total += third_in[i, low : low + m].astype(F32)
        spot = starts[p] + at[orders[p][0]] * (4 * m) + at[orders[p][1]] * m
        out_ref[core, pl.ds(spot, m)] = total.astype(BF16)
        live[p] = exchange(
            3, p, orders[p][1],
            lambda other, i, spot=spot, m=m: out_ref.at[core, pl.ds(spot, m)],
            lambda i, spot=spot, m=m: out_ref.at[core, pl.ds(spot, m)],
        )
    for p in range(3):
        m = share[p]
        finish(live[p])
        spot = starts[p] + at[orders[p][0]] * (4 * m)
        live[p] = exchange(
            4, p, orders[p][0],
            lambda other, i, spot=spot, m=m: out_ref.at[core, pl.ds(spot, 4 * m)],
            lambda i, spot=spot, m=m: out_ref.at[core, pl.ds(spot, 4 * m)],
        )
    last = []
    for p in range(3):
        finish(live[p])
        spot, m = starts[p], 16 * share[p]
        last.append(pltpu.make_async_remote_copy(
            src_ref=out_ref.at[core, pl.ds(spot, m)], dst_ref=out_ref.at[core, pl.ds(spot, m)],
            send_sem=core_sem.at[2 + p], recv_sem=core_sem.at[5 + p],
            device_id=sibling, device_id_type=MESH,
        ))
        last[-1].start()
    finish(returns)
    finish(last)


def sum_call(bands, sectors, back, grads):
    half = grads.shape[0] // 2
    unit = half // 16
    share = (unit - 2 * (unit // 3), unit // 3, unit // 3)
    whole = pl.BlockSpec(memory_space=pltpu.VMEM)
    there = pl.BlockSpec(memory_space=pl.ANY)
    tile = grads.shape[1:]
    return pl.pallas_call(
        functools.partial(sum_kernel, bands, sectors, share),
        in_specs=[there, there],
        out_specs=[there, whole],
        out_shape=[
            jax.ShapeDtypeStruct(back.shape, BF16),
            jax.ShapeDtypeStruct((2, half) + tile, BF16),
        ],
        scratch_shapes=[
            pltpu.VMEM((half,) + tile, BF16),
            pltpu.VMEM((half,) + tile, BF16),
            pltpu.VMEM((half // 4,) + tile, BF16),
            pltpu.VMEM((unit,) + tile, BF16),
            pltpu.VMEM((3, half // 4) + tile, BF16),
            pltpu.VMEM((3, unit) + tile, BF16),
            pltpu.VMEM((4, unit) + tile, BF16),
            pltpu.VMEM((half,) + tile, BF16),
            pltpu.SemaphoreType.DMA((5, 3, 3)),
            pltpu.SemaphoreType.DMA((5, 3, 3)),
            pltpu.SemaphoreType.DMA((8,)),
            pltpu.SemaphoreType.DMA((8,)),
            pltpu.SemaphoreType.DMA((8,)),
            pltpu.SemaphoreType.DMA,
        ],
        compiler_params=pltpu.CompilerParams(
            collective_id=1, has_side_effects=True, vmem_limit_bytes=60 * 1024 * 1024
        ),
    )(back, grads.reshape((2, half) + tile))


def close_kernel(scale, rows_ref, arrived_hbm, part_hbm, sums_hbm, *refs):
    targets, (arrived_ref, part_ref, sums_ref, ngrad_ref), outs = refs[:5], refs[5:9], refs[9:13]
    load_sem, store_sem = refs[13:]
    spans, at = [], 0
    for out in outs:
        size = out.shape[0] // 8
        spans.append((at, size))
        at += size
    loads = [
        pltpu.make_async_copy(sums_hbm.at[start : start + size], sums_ref.at[start : start + size], load_sem.at[i])
        for i, (start, size) in enumerate(spans)
    ]
    loads.append(pltpu.make_async_copy(part_hbm, part_ref, load_sem.at[4]))
    loads.append(pltpu.make_async_copy(arrived_hbm, arrived_ref, load_sem.at[5]))
    for load in loads:
        load.start()
    stores = [
        pltpu.make_async_copy(ref, target, store_sem.at[i])
        for i, (ref, target) in enumerate(zip(outs + (ngrad_ref,), targets[1:] + targets[:1]))
    ]
    n = part_ref.shape[0]
    chosen = [picked(rows_ref[0, j : j + 1, :], n) for j in range(8)]
    for i, (out, (start, size)) in enumerate(zip(outs, spans)):
        loads[i].wait()
        for tile in range(size):
            r, l = 16 * (tile // 2), 128 * (tile % 2)
            out[r : r + 16, l : l + 128] = sums_ref[start + tile].astype(F32) * scale
        stores[i].start()
    loads[4].wait()
    loads[5].wait()
    total = part_ref[...]
    for j in range(8):
        total += dot(chosen[j], arrived_ref[j])
    ngrad_ref[...] = total
    stores[4].start()
    for store in stores:
        store.wait()


def close_call(scale, rows, arrived, part, sums):
    d = part.shape[1]
    whole = pl.BlockSpec(memory_space=pltpu.VMEM)
    there = pl.BlockSpec(memory_space=pl.ANY)
    outs = [part.shape, (3 * d, d), (d, d), (2 * d, d), (d, d)]
    sums = sums.reshape((-1,) + sums.shape[2:])
    return pl.pallas_call(
        functools.partial(close_kernel, scale),
        in_specs=[whole, there, there, there],
        out_specs=[there] * 5,
        out_shape=[jax.ShapeDtypeStruct(shape, F32) for shape in outs],
        scratch_shapes=[
            pltpu.VMEM(arrived.shape, BF16),
            pltpu.VMEM(part.shape, F32),
            pltpu.VMEM(sums.shape, BF16),
        ]
        + [pltpu.VMEM(shape, F32) for shape in outs]
        + [pltpu.SemaphoreType.DMA((6,)), pltpu.SemaphoreType.DMA((5,))],
        compiler_params=pltpu.CompilerParams(vmem_limit_bytes=60 * 1024 * 1024),
    )(rows, arrived, part, sums)


def solution(mesh):
    bands, sectors = mesh.shape["band"], mesh.shape["sector"]

    def local(node, edge, slot, mask, rows, w_ein, b_e, w_eout, g_e, w_nin, b_n, w_nout, g_n, ncot, ecot):
        n, d = node.shape
        far = fetch_call(bands, sectors, node, rows)
        nnew, enew, egrad, part, back, grads = layer_call(
            node, far.reshape(-1, d), edge, slot, mask,
            w_ein, b_e, w_eout, g_e, w_nin, b_n, w_nout, g_n, ncot, ecot,
        )
        arrived, sums = sum_call(bands, sectors, back, grads)
        scale = float(bands * sectors * n * slot.shape[1]) ** (-0.5)
        outs = close_call(scale, rows, arrived, part, sums)
        return (nnew, enew, outs[0], egrad) + tuple(outs[1:])

    split = P(("band", "sector"), None)
    in_specs = (split,) * 4 + (P(("band", "sector"), None, None),) + (P(),) * 8 + (split, split)
    out_specs = (split,) * 4 + (P(),) * 4
    return jax.shard_map(local, mesh=mesh, in_specs=in_specs, out_specs=out_specs, check_vma=False)
```
